512 devices in a mesh: grp: 16 (over y, z_hi, core), sub: 32 (over x, z_lo).
Axes of the slice: x: 4, y: 4, z: 16 (z_hi: 2, z_lo: 8; z = z_hi * 8 + z_lo), core: 2. Of those that a mesh axis runs over, the one named last changes fastest.
Arguments:
- activations: bfloat16 [262144, 2048], P(('grp', 'sub')), may hold values from -110 to 110
- norm_gain: float32 [2048], replicated, may hold values from 0.5 to 1.5
- key_weight: bfloat16 [2048, 768], P('sub'), may hold values from -0.125 to 0.125
- key_grads: bfloat16 [262144, 768], P(('grp', 'sub')), may hold values from -3 to 3
Outputs:
- input_grads: bfloat16 [262144, 2048], P(('grp', 'sub'))
- weight_grads: float32 [2048, 768], P('sub', 'grp')
- gain_grads: float32 [2048], P('sub')
The draws below stay inside these ranges and needn't reach their ends.
All inputs are finite; a program needn't handle non-finite values.
Results may differ from the reference program's by a relative error of at most 0.0029.
Values may be sent and summed in bfloat16 or wider, within the bound.
A program may use at most 64 MiB of HBM per device.

```python
import math
import jax
import jax.numpy as jnp
from jax import lax

D = 2048
KW = 768
TOK_DEV = 512
TOKENS = 262144
N_GRP = 16
N_SUB = 32


def draw_activations(key, part):
    key_base, key_rows, key_cols = jax.random.split(key, 3)
    base = jnp.clip(jax.random.normal(key_base, (TOKENS, D), jnp.float32), -4.0, 4.0)
    row_scale = jnp.exp(jax.random.uniform(key_rows, (TOKENS, 1), jnp.float32) * math.log(10.0))
    col_scale = 0.5 * jnp.exp(jax.random.uniform(key_cols, (1, D), jnp.float32) * math.log(4.0))
    return (base * row_scale * col_scale).astype(jnp.bfloat16)


def levels(rng, extent, pieces, least, high):
    level, own = 1.0, jax.random.fold_in(rng, 6)
    for dim, parts in pieces:
        steps = jnp.exp(jax.random.uniform(jax.random.fold_in(own, dim), (parts,), jnp.float32, least / len(pieces), high / len(pieces)))
        level = level * jnp.repeat(steps, extent[dim] // parts).reshape([-1 if axis == dim else 1 for axis in range(len(extent))])
    return level


def scatter_about(key, dims, deviation, bound, shards=(), dtype=jnp.bfloat16):
    entries = deviation * jax.random.normal(key, dims, jnp.float32)
    if shards:
        entries = entries * levels(key, dims, shards, -0.22, 0.18)
    return jnp.clip(entries, -bound, bound).astype(dtype)


def setup_inputs(seed: int = 0) -> dict:
    seeds = jax.random.split(jax.random.key(seed), 5)
    activations = draw_activations(jax.random.fold_in(seeds[4], 71), 0)
    norm_gain = jnp.clip(jax.random.uniform(seeds[1], (D,), jnp.float32, 0.5, 1.5), 0.5, 1.5)
    key_weight = scatter_about(seeds[2], (D, KW), D ** -0.5, 0.125, ((0, 32),))
    key_grads = scatter_about(seeds[3], (TOKENS, KW), 0.5, 3.0, ((0, 512),))
    return {"activations": activations, "norm_gain": norm_gain, "key_weight": key_weight, "key_grads": key_grads}


def reference(activations, norm_gain, key_weight, key_grads):
    inputs = activations.astype(jnp.float32)
    mean_square = lax.optimization_barrier(jnp.mean(inputs * inputs, axis=1, keepdims=True))
    inverse_rms = lax.rsqrt(mean_square + 1e-05)
    normed = inputs * inverse_rms
    scaled = (normed * norm_gain).astype(jnp.bfloat16)
    grad_scaled = jnp.dot(key_grads, key_weight.T, preferred_element_type=jnp.float32)
    gained = norm_gain * grad_scaled
    input_grads = (inverse_rms * (gained - normed * lax.optimization_barrier(jnp.mean(gained * normed, axis=1, keepdims=True)))).astype(jnp.bfloat16)
    groups = N_GRP
    gain_grads = lax.optimization_barrier(jnp.sum(grad_scaled * normed, axis=0)) / groups
    blocks = N_GRP * N_SUB
    scaled_blocks = scaled.reshape(blocks, TOK_DEV, D)
    grad_blocks = key_grads.reshape(blocks, TOK_DEV, KW)

    def add_block(total, pair):
        block_rows, block_grads = pair
        term = jnp.dot(block_rows.T, block_grads, preferred_element_type=jnp.float32)
        return (total + term, None)
    total, unused = lax.scan(add_block, jnp.zeros((D, KW), jnp.float32), (scaled_blocks, grad_blocks))
    weight_grads = total / groups
    return (input_grads, weight_grads, gain_grads)
```

```python
import functools

import jax
import jax.numpy as jnp
from jax import lax
from jax.experimental import pallas as pl
from jax.experimental.pallas import tpu as pltpu
from jax.sharding import PartitionSpec as P

MESH = pl.DeviceIdType.MESH
F32 = jnp.float32
BF16 = jnp.bfloat16
NX, NY, NZL, NZH = 4, 4, 8, 2
NZ = NZL * NZH
ORDER = (0, 1, 3, 2)


def kernel(
    act, gain, weight, grads,
    out, tail,
    scaled, inv, grads_t, w, t32, p_send, p_recv, p, rs_a, rs_b, rs_c, rs_d, rs_e, rs_f, q, u, u_send, u_recv,
    v, z_send, z_recv, lg, g_own, g_part, g_x, g_y,
    send, agz, ag1, ag2l, ag2r, agfl, agfr, agp, rsp, rs1, rs2, zsem, gp, gx, gy,
):
    g_idx, s_idx = lax.axis_index("grp"), lax.axis_index("sub")
    core = lax.rem(g_idx, 2)
    zh = lax.rem(lax.div(g_idx, 2), 2)
    y = lax.div(g_idx, 4)
    x = lax.div(s_idx, NZL)
    zl = lax.rem(s_idx, NZL)
    z = zh * NZL + zl
    f = x + core * (y - x)
    s = y + core * (x - y)
    tokens, model = act.shape
    key = grads.shape[1]

    def dev(dx, dy, dz, dc):
        return ((dy * 2 + lax.div(dz, NZL)) * 2 + dc, dx * NZL + lax.rem(dz, NZL))

    def xy(df, ds):
        return df + core * (ds - df), ds + core * (df - ds)

    def dev_fs(df, ds):
        dx, dy = xy(df, ds)
        return dev(dx, dy, z, core)

    def m4(a):
        return lax.rem(a, 4)

    partner = dev(x, y, z, 1 - core)
    right, left = m4(f + 1), m4(f + 3)
    s_right, s_left = m4(s + 1), m4(s + 3)

    sent = []

    def copy(src, dst, recv, device):
        return pltpu.make_async_remote_copy(
            src_ref=src, dst_ref=dst, send_sem=send.at[len(sent)], recv_sem=recv,
            device_id=device, device_id_type=MESH,
        )

    def go(src, dst, recv, device):
        made = copy(src, dst, recv, device)
        made.start()
        sent.append(made)

    def got(dst, recv, device):
        pltpu.make_async_remote_copy(
            src_ref=dst, dst_ref=dst, send_sem=send.at[0], recv_sem=recv,
            device_id=device, device_id_type=MESH,
        ).wait_recv()

    barrier = pltpu.get_barrier_semaphore()
    peers = [partner]
    peers += [dev(m4(x + k), y, z, core) for k in range(1, NX)]
    peers += [dev(x, m4(y + k), z, core) for k in range(1, NY)]
    peers += [dev(x, y, lax.rem(z + k, NZ), core) for k in range(1, NZ)]
    for peer in peers:
        pl.semaphore_signal(barrier, inc=1, device_id=peer, device_id_type=MESH)

    rows = 64

    @pl.loop(0, tokens // rows)
    def _(i):
        block = pl.ds(pl.multiple_of(i * rows, rows), rows)
        a = act[block, :].astype(F32)
        r = lax.rsqrt(jnp.sum(a * a, axis=1, keepdims=True) * (1.0 / model) + 1e-05)
        inv[block, :] = jnp.broadcast_to(r, (rows, 128))
        scaled[block, :] = (a * r * gain[...]).astype(BF16)

    grads_t[...] = grads[...].T.reshape(16, 48, tokens)

    pl.semaphore_wait(barrier, len(peers))

    half = 4 * core
    mine = lax.div(zl, 4) == core
    z_offsets = (1, 15, 2, 14, 3, 13, 4)

    @pl.when(mine)
    def _():
        w[x, zl, y] = weight[y]

    def z_copy(n, off):
        return pltpu.make_async_remote_copy(
            src_ref=weight.at[y], dst_ref=w.at[x, zl, y],
            send_sem=send.at[n], recv_sem=agz.at[lax.rem(zl, 4)],
            device_id=dev(x, y, lax.rem(z + off, NZ), core), device_id_type=MESH,
        )

    @pl.when(mine)
    def _():
        for n, off in enumerate(z_offsets):
            z_copy(n, off).start()

    sent.extend([None] * len(z_offsets))

    def product(parity, i):
        lhs = jnp.concatenate([grads_t[2 * j + parity] for j in range(8)], axis=0)
        rhs = scaled[:, pl.ds(pl.multiple_of(i * 512, 512), 512)]
        return jnp.dot(lhs, rhs, preferred_element_type=F32).reshape(8, 48, 512)

    first = len(sent)

    def p_copy(i):
        return pltpu.make_async_remote_copy(
            src_ref=p_send.at[i], dst_ref=p_recv.at[i], send_sem=send.at[first + i],
            recv_sem=rsp.at[i], device_id=partner, device_id_type=MESH,
        )

    @pl.loop(0, NX)
    def _(i):
        p_send[i] = product(1 - core, i).astype(BF16)
        p_copy(i).start()

    sent.extend(p_copy(i) for i in range(NX))

    @pl.loop(0, NX)
    def _(i):
        t32[i] = product(core, i)

    def piece(df, ds):
        dx, dy = xy(df, ds)
        return w.at[dx, pl.ds(half, 4), dy]

    def pass_on(k, ds):
        at = piece(m4(f + k), ds)
        go(at, at, agp, partner)

    def spread(k):
        at = piece(m4(f + k), s)
        go(at, at, ag2l.at[k], dev_fs(f, s_right))
        go(at, at, ag2r.at[k], dev_fs(f, s_left))

    for i in range(4):
        @pl.when(half + i != zl)
        def _():
            got(w.at[x, half + i, y], agz.at[i], partner)

    own = piece(f, s)
    for k in (1, 3, 2):
        go(own, own, ag1.at[4 - k], dev_fs(m4(f + k), s))
    spread(0)
    pass_on(0, s)

    @pl.loop(0, NX)
    def _(i):
        p_copy(i).wait_recv()
        for dy in range(NY):
            df, ds = xy(i, dy)
            for dz in range(NZH):
                total = t32[i, 2 * dy + dz] + p_recv[i, 2 * dy + dz].astype(F32)
                t32[i, 2 * dy + dz] = total
                p[df, ds, dz] = total.astype(BF16)

    for k in (1, 3, 2):
        got(piece(m4(f + k), s), ag1.at[k], dev_fs(m4(f + k), s))
        spread(k)
        pass_on(k, s)

    def part(df, h):
        return p.at[m4(df), pl.ds(2 * h, 2)]

    to_right, to_left = dev_fs(right, s), dev_fs(left, s)
    go(part(f + 2, 0), rs_a, rs1.at[0], to_right)
    go(part(f + 2, 1), rs_c, rs1.at[2], to_left)
    go(part(f + 1, 1), rs_b, rs1.at[1], to_right)
    go(part(f + 3, 0), rs_d, rs1.at[3], to_left)

    for k in ORDER:
        got(piece(m4(f + k), s_left), ag2l.at[k], dev_fs(f, s_left))
        if k in ORDER[:2]:
            at = piece(m4(f + k), s_left)
            go(at, at, agfl.at[k], dev_fs(f, s_right))
        pass_on(k, s_left)
        got(piece(m4(f + k), s_right), ag2r.at[k], dev_fs(f, s_right))
        if k in ORDER[2:]:
            at = piece(m4(f + k), s_right)
            go(at, at, agfr.at[k], dev_fs(f, s_left))
        pass_on(k, s_right)

    def term(df, ds, dz):
        dx, dy = xy(df, ds)
        return t32[dx, 2 * dy + dz]

    got(rs_a, rs1.at[0], to_left)
    for i in range(2):
        for dz in range(NZH):
            q[0, i, dz] = (term(right, i, dz) + rs_a[i, dz].astype(F32)).astype(BF16)
    go(q.at[0], rs_e, rs1.at[4], to_right)
    got(rs_c, rs1.at[2], to_right)
    for i in range(2):
        for dz in range(NZH):
            q[1, i, dz] = (term(left, 2 + i, dz) + rs_c[i, dz].astype(F32)).astype(BF16)
    go(q.at[1], rs_f, rs1.at[5], to_left)

    opposite = m4(s + 2)
    for k in ORDER[:2]:
        got(piece(m4(f + k), opposite), agfl.at[k], dev_fs(f, s_left))
        pass_on(k, opposite)
    for k in ORDER[2:]:
        got(piece(m4(f + k), opposite), agfr.at[k], dev_fs(f, s_right))
        pass_on(k, opposite)

    got(rs_d, rs1.at[3], to_right)
    got(rs_e, rs1.at[4], to_left)
    got(rs_b, rs1.at[1], to_left)
    got(rs_f, rs1.at[5], to_right)
    for i in range(2):
        for dz in range(NZH):
            u[i, dz] = term(f, i, dz) + rs_d[i, dz].astype(F32) + rs_e[i, dz].astype(F32)
            u_send[i, dz] = u[i, dz].astype(BF16)
            u[2 + i, dz] = term(f, 2 + i, dz) + rs_b[i, dz].astype(F32) + rs_f[i, dz].astype(F32)
            u_send[2 + i, dz] = u[2 + i, dz].astype(BF16)
    for k in (1, 3, 2):
        go(u_send.at[m4(s + k)], u_recv.at[4 - k], rs2.at[4 - k], dev_fs(f, m4(s + k)))

    far = pl.ds(4 - half, 4)
    got(w.at[:, far], agp, partner)
    weight_all = w[...].reshape(model, key)
    lg[...] = jnp.zeros_like(lg)
    rows2 = 64

    @pl.loop(0, tokens // rows2)
    def _(i):
        block = pl.ds(pl.multiple_of(i * rows2, rows2), rows2)
        grad = lax.dot_general(
            grads[block, :], w[...].reshape(model, key), (((1,), (1,)), ((), ())),
            preferred_element_type=F32,
        )
        r = inv[block, :][:, :1]
        normed = act[block, :].astype(F32) * r
        both = grad * normed
        lg[...] += jnp.sum(both.reshape(rows2 // 8, 8, model), axis=0)
        mean = jnp.sum(both * gain[...], axis=1, keepdims=True) * (1.0 / model)
        out[block, :] = (r * (gain[...] * grad - normed * mean)).astype(BF16)

    line = jnp.sum(lg[...], axis=0, keepdims=True)
    for j in range(model // 128):
        g_own[j : j + 1, :] = line[:, 128 * j : 128 * (j + 1)]
    go(g_own, g_part, gp, partner)
    got(g_part, gp, partner)
    g_x[x] = g_own[...] + g_part[...]
    for k in range(1, NX):
        go(g_x.at[x], g_x.at[x], gx.at[4 - k], dev(m4(x + k), y, z, core))

    for k in range(1, 4):
        got(u_recv.at[k], rs2.at[k], dev_fs(f, m4(s + k)))
    for dz in range(NZH):
        v[dz] = (
            (u[s, dz] + u_recv[1, dz].astype(F32))
            + (u_recv[2, dz].astype(F32) + u_recv[3, dz].astype(F32))
        )

    for k in range(1, NX):
        got(g_x.at[m4(x + k)], gx.at[k], dev(m4(x + k), y, z, core))
    g_y[y] = (g_x[0] + g_x[1]) + (g_x[2] + g_x[3])
    for k in range(1, NY):
        go(g_y.at[y], g_y.at[y], gy.at[4 - k], dev(x, m4(y + k), z, core))

    lane = lax.broadcasted_iota(jnp.int32, (24, 128), 1)
    for dz in range(NZH):
        for pair in range(NZL // 2):
            top = v[dz, 0:24, 128 * pair : 128 * (pair + 1)]
            low = v[dz, 24:48, 128 * pair : 128 * (pair + 1)]
            z_send[dz * NZL + 2 * pair, 0:24] = jnp.where(lane < 64, top, pltpu.roll(low, 64, 1))
            z_send[dz * NZL + 2 * pair + 1, 0:24] = jnp.where(lane < 64, pltpu.roll(top, 64, 1), low)
    for k in range(1, NY):
        got(g_y.at[m4(y + k)], gy.at[k], dev(x, m4(y + k), z, core))
    g_own_xy = [(g_y[0, pl.ds(4 * x + pair, 1)] + g_y[1, pl.ds(4 * x + pair, 1)])
                + (g_y[2, pl.ds(4 * x + pair, 1)] + g_y[3, pl.ds(4 * x + pair, 1)]) for pair in range(NZL // 2)]
    for dz in range(NZ):
        z_send[dz, 24:32] = jnp.broadcast_to(g_own_xy[(dz % NZL) // 2], (8, 128))
    for k in range(1, NZ):
        there = lax.rem(z + k, NZ)
        go(z_send.at[there], z_recv.at[z], zsem.at[NZ - k], dev(x, y, there, core))
    z_recv[z] = z_send[z]
    for k in range(1, NZ):
        there = lax.rem(z + k, NZ)
        got(z_recv.at[there], zsem.at[k], dev(x, y, there, core))
    total = z_recv[0]
    for k in range(1, NZ):
        total = total + z_recv[k]
    total = total * (1.0 / 16)
    tail[0:24] = total[0:24]
    tail[24:32] = jnp.where(lax.rem(zl, 2) == 1, pltpu.roll(total[24:32], 64, 1), total[24:32])

    @pl.when(mine)
    def _():
        for n, off in enumerate(z_offsets):
            z_copy(n, off).wait_send()

    for made in sent:
        if made is not None:
            made.wait_send()


def local(activations, norm_gain, key_weight, key_grads):
    tokens, model = activations.shape
    key = key_grads.shape[1]
    dma = pltpu.SemaphoreType.DMA
    half_chunk = pltpu.VMEM((2, NZH, 48, 512), BF16)
    scratch = [
        pltpu.VMEM((tokens, model), BF16),
        pltpu.VMEM((tokens, 128), F32),
        pltpu.VMEM((16, 48, tokens), BF16),
        pltpu.VMEM((NX, NZL, 4, 16, key), BF16),
        pltpu.VMEM((NX, 8, 48, 512), F32),
        pltpu.VMEM((NX, 8, 48, 512), BF16),
        pltpu.VMEM((NX, 8, 48, 512), BF16),
        pltpu.VMEM((4, 4, NZH, 48, 512), BF16),
        half_chunk, half_chunk, half_chunk, half_chunk, half_chunk, half_chunk,
        pltpu.VMEM((2, 2, NZH, 48, 512), BF16),
        pltpu.VMEM((4, NZH, 48, 512), F32),
        pltpu.VMEM((4, NZH, 48, 512), BF16),
        pltpu.VMEM((4, NZH, 48, 512), BF16),
        pltpu.VMEM((NZH, 48, 512), F32),
        pltpu.VMEM((NZ, 32, 128), F32),
        pltpu.VMEM((NZ, 32, 128), F32),
        pltpu.VMEM((8, model), F32),
        pltpu.VMEM((16, 128), F32),
        pltpu.VMEM((16, 128), F32),
        pltpu.VMEM((NX, 16, 128), F32),
        pltpu.VMEM((NY, 16, 128), F32),
        dma((96,)),
        dma((4,)),
        dma((4,)), dma((4,)), dma((4,)), dma((4,)), dma((4,)),
        dma,
        dma((NX,)),
        dma((6,)),
        dma((4,)),
        dma((NZ,)),
        dma,
        dma((4,)),
        dma((4,)),
    ]
    vmem = pl.BlockSpec(memory_space=pltpu.VMEM)
    input_grads, tail = pl.pallas_call(
        kernel,
        out_shape=(
            jax.ShapeDtypeStruct((tokens, model), BF16),
            jax.ShapeDtypeStruct((32, 128), F32),
        ),
        in_specs=[vmem] * 4,
        out_specs=(vmem, vmem),
        scratch_shapes=scratch,
        compiler_params=pltpu.CompilerParams(
            collective_id=0, has_side_effects=True, vmem_limit_bytes=60 * 1024 * 1024
        ),
    )(activations, norm_gain.reshape(1, model), key_weight.reshape(4, 16, key), key_grads)
    packed = tail[:24]
    weight_grads = jnp.concatenate([packed[:, :64], packed[:, 64:]], axis=0).T
    return input_grads, weight_grads, tail[24, :64]


def solution(mesh):
    return jax.shard_map(
        local,
        mesh=mesh,
        in_specs=(P(("grp", "sub"), None), P(), P("sub", None), P(("grp", "sub"), None)),
        out_specs=(P(("grp", "sub"), None), P("sub", "grp"), P("sub")),
        check_vma=False,
    )
```

```python
import functools

import jax
import jax.numpy as jnp
from jax import lax
from jax.experimental import pallas as pl
from jax.experimental.pallas import tpu as pltpu
from jax.sharding import PartitionSpec as P

MESH = pl.DeviceIdType.MESH
F32 = jnp.float32
BF16 = jnp.bfloat16
NX, NY, NZL, NZH = 4, 4, 8, 2
NZ = NZL * NZH
Z_ORDER = (8, 7, 9, 6, 10, 5, 11, 4, 12, 3, 13, 2, 14, 1, 15)
S_Z, S_P, S_W, S_PASS, S_ZP, S_RS1, S_RS2, S_ZT, S_GX, S_GY, S_GZ = range(11)


def kernel(
    act_hbm, gain_hbm, weight, grads_hbm,
    out, tail,
    act, gain, grads, gs, row_sum, scaled, inv, grads_t, w, t_give, t_keep, p_send, p_recv, give, given, p, r1, u, u_recv,
    v, z_send, z_recv, lg, g_x, g_y, gz_send, gz_recv,
    load, send, agz, ag1, ag2l, ag2r, agfl, agfr, agp, rsp, rsz, rs1, rs2, zsem, gx, gy, gz,
):
    g_idx, s_idx = lax.axis_index("grp"), lax.axis_index("sub")
    core = lax.rem(g_idx, 2)
    zh = lax.rem(lax.div(g_idx, 2), 2)
    y = lax.div(g_idx, 4)
    x = lax.div(s_idx, NZL)
    zl = lax.rem(s_idx, NZL)
    z = zh * NZL + zl
    f = x + core * (y - x)
    s = y + core * (x - y)
    tokens, model = act.shape
    key = grads.shape[1]

    def dev(dx, dy, dz, dc):
        return ((dy * 2 + lax.div(dz, NZL)) * 2 + dc, dx * NZL + lax.rem(dz, NZL))

    def xy(df, ds):
        return df + core * (ds - df), ds + core * (df - ds)

    def dev_fs(df, ds):
        dx, dy = xy(df, ds)
        return dev(dx, dy, z, core)

    def m4(a):
        return lax.rem(a, 4)

    partner = dev(x, y, z, 1 - core)
    right, left = m4(f + 1), m4(f + 3)
    s_right, s_left = m4(s + 1), m4(s + 3)

    def go(src, dst, group, recv, device):
        pltpu.make_async_remote_copy(
            src_ref=src, dst_ref=dst, send_sem=send.at[group], recv_sem=recv,
            device_id=device, device_id_type=MESH,
        ).start()

    def left_here(ref, group):
        pltpu.make_async_remote_copy(
            src_ref=ref, dst_ref=ref, send_sem=send.at[group], recv_sem=send.at[group],
            device_id=partner, device_id_type=MESH,
        ).wait_send()

    def got(dst, recv, device):
        pltpu.make_async_remote_copy(
            src_ref=dst, dst_ref=dst, send_sem=send.at[0], recv_sem=recv,
            device_id=device, device_id_type=MESH,
        ).wait_recv()

    barrier = pltpu.get_barrier_semaphore()
    peers = [partner]
    peers += [dev(m4(x + k), y, z, core) for k in range(1, NX)]
    peers += [dev(m4(x + k), y, z, 1 - core) for k in range(1, NX)]
    peers += [dev(x, m4(y + k), z, core) for k in range(1, NY)]
    peers += [dev(x, y, lax.rem(z + k, NZ), core) for k in range(1, NZ)]
    for peer in peers:
        pl.semaphore_signal(barrier, inc=1, device_id=peer, device_id_type=MESH)

    quarter = tokens // 4
    loads = [
        pltpu.make_async_copy(
            act_hbm.at[pl.ds(i * quarter, quarter)], act.at[pl.ds(i * quarter, quarter)], load.at[i]
        )
        for i in range(4)
    ]
    loads.append(pltpu.make_async_copy(gain_hbm, gain, load.at[4]))
    loads.append(pltpu.make_async_copy(grads_hbm, grads, load.at[5]))
    for i in (4, 0, 1, 2, 3, 5):
        loads[i].start()

    pl.semaphore_wait(barrier, len(peers))

    half = 4 * core
    mine = lax.div(zl, 4) == core
    z_offsets = (4, 3, 13, 2, 14, 1, 15)

    own_rows = pltpu.make_async_copy(weight.at[y], w.at[x, zl, y], load.at[6])

    @pl.when(mine)
    def _():
        for off in z_offsets:
            to = dev(x, y, lax.rem(z + off, NZ), core)
            go(weight.at[y], w.at[x, zl, y], S_Z, agz.at[lax.rem(zl, 4)], to)
        own_rows.start()

    rows = 64
    loads[4].wait()

    @pl.loop(0, tokens // rows)
    def _(i):
        @pl.when(lax.rem(i, 2) == 0)
        def _():
            at = pl.ds(pl.multiple_of(lax.div(i, 2) * quarter, quarter), quarter)
            pltpu.make_async_copy(act_hbm.at[at], act.at[at], load.at[lax.div(i, 2)]).wait()

        block = pl.ds(pl.multiple_of(i * rows, rows), rows)
        a = act[block, :].astype(F32)
        r = lax.rsqrt(jnp.sum(a * a, axis=1, keepdims=True) * (1.0 / model) + 1e-05)
        inv[block, :] = jnp.broadcast_to(r, (rows, 128))
        scaled[block, :] = (a * r * gain[...]).astype(BF16)

    loads[5].wait()
    grads_t[...] = grads[...].T.reshape(16, 48, tokens)

    keep_half = lax.rem(z, 2)
    half_keep = 4 * keep_half
    to_self = lax.div(zl, 4) == keep_half
    up, down = dev(x, y, lax.rem(z + 1, NZ), core), dev(x, y, lax.rem(z + NZ - 1, NZ), core)

    def product(parity, i, side):
        lhs = jnp.concatenate([grads_t[2 * j + parity] for j in range(8)], axis=0)
        rhs = scaled[:, pl.ds(pl.multiple_of(i * 512 + side * 256, 256), 256)]
        return jnp.dot(lhs, rhs, preferred_element_type=F32).reshape(8, 48, 256)

    def for_partner(n, side):
        @pl.loop(0, NX)
        def _(i):
            p_send[n, i] = product(1 - core, i, side).astype(BF16)
            go(p_send.at[n, i], p_recv.at[n, i], S_P, rsp.at[NX * n + i], partner)

    for_partner(0, 1 - keep_half)

    @pl.loop(0, NX)
    def _(i):
        t_give[i] = product(core, i, 1 - keep_half)

    @pl.loop(0, NX)
    def _(i):
        got(p_recv.at[0, i], rsp.at[i], partner)
        for j in range(8):
            give[i, j] = (t_give[i, j] + p_recv[0, i, j].astype(F32)).astype(BF16)
        go(give.at[i, pl.ds(0, 4)], given.at[i, pl.ds(0, 4)], S_ZP, rsz.at[i], up)
        go(give.at[i, pl.ds(4, 4)], given.at[i, pl.ds(4, 4)], S_ZP, rsz.at[NX + i], down)

    for_partner(1, keep_half)

    @pl.loop(0, NX)
    def _(i):
        t_keep[i] = product(core, i, keep_half)


    def piece(df, ds):
        dx, dy = xy(df, ds)
        return w.at[dx, pl.ds(half, 4), dy]

    def pass_on(k, ds):
        at = piece(m4(f + k), ds)
        go(at, at, S_PASS, agp.at[xy(m4(f + k), ds)[0]], partner)

    to_right, to_left = dev_fs(right, s), dev_fs(left, s)
    to_s_right, to_s_left = dev_fs(f, s_right), dev_fs(f, s_left)
    opposite = m4(s + 2)

    def spread(k):
        at = piece(m4(f + k), s)
        go(at, at, S_W, ag2l.at[k], to_s_right)
        go(at, at, S_W, ag2r.at[k], to_s_left)

    for i in range(4):
        @pl.when(half + i != zl)
        def _():
            got(w.at[x, half + i, y], agz.at[i], partner)

    @pl.when(mine)
    def _():
        own_rows.wait()

    own = piece(f, s)
    for k in (1, 3, 2):
        go(own, own, S_W, ag1.at[4 - k], dev_fs(m4(f + k), s))
    spread(0)
    pass_on(0, s)

    @pl.loop(0, NX)
    def _(i):
        got(p_recv.at[1, i], rsp.at[NX + i], partner)
        for j in range(8):
            t_keep[i, j] += p_recv[1, i, j].astype(F32)

    def first_axis(k):
        got(piece(m4(f + k), s), ag1.at[k], dev_fs(m4(f + k), s))
        spread(k)
        if k == 2:
            at = piece(m4(f + k), s)
            go(at, at, S_W, agfr.at[2], dev_fs(f, opposite))
        pass_on(k, s)

    def second_axis(k):
        at = piece(m4(f + k), s_left)
        got(at, ag2l.at[k], to_s_left)
        if k in (0, 1):
            go(at, at, S_W, agfl.at[k], to_s_right)
        pass_on(k, s_left)
        at = piece(m4(f + k), s_right)
        got(at, ag2r.at[k], to_s_right)
        if k == 3:
            go(at, at, S_W, agfr.at[k], to_s_left)
        pass_on(k, s_right)

    def across(k):
        sem, device = {
            0: (agfl, to_s_left), 1: (agfl, to_s_left), 3: (agfr, to_s_right), 2: (agfr, dev_fs(f, opposite)),
        }[k]
        got(piece(m4(f + k), opposite), sem.at[k], device)
        pass_on(k, opposite)

    first_axis(1)
    first_axis(3)
    second_axis(0)
    first_axis(2)

    @pl.loop(0, NX)
    def _(i):
        got(given.at[i, pl.ds(0, 4)], rsz.at[i], down)
        got(given.at[i, pl.ds(4, 4)], rsz.at[NX + i], up)
        for dy in range(NY):
            df, ds = xy(i, dy)
            for dz in range(NZH):
                total = t_keep[i, 2 * dy + dz] + given[i, 2 * dy + dz].astype(F32)
                t_keep[i, 2 * dy + dz] = total
                p[df, ds, dz] = total.astype(BF16)

    for k in (1, 3, 2):
        go(p.at[m4(f + k)], r1.at[3 - k], S_RS1, rs1, dev_fs(m4(f + k), s))

    second_axis(1)
    second_axis(3)
    across(0)

    far = pl.ds(4 - half, 4)
    rows2 = 256
    lg[...] = jnp.zeros_like(lg)
    row_sum[...] = jnp.zeros_like(row_sum)

    def features(dx):
        got(w.at[dx, far], agp.at[dx], partner)
        columns = pl.ds(pl.multiple_of(dx * 512, 512), 512)

        @pl.loop(0, tokens // rows2)
        def _(i):
            block = pl.ds(pl.multiple_of(i * rows2, rows2), rows2)
            grad = lax.dot_general(
                grads[block, :], w[dx].reshape(512, key), (((1,), (1,)), ((), ())),
                preferred_element_type=F32,
            )
            gs[block, columns] = grad
            both = grad * (act[block, columns].astype(F32) * inv[block, :][:, :1])
            lg[:, columns] += jnp.sum(both.reshape(rows2 // 8, 8, 512), axis=0)
            both = both * gain[:, columns]
            row_sum[block, :] += (both[:, 0:128] + both[:, 128:256]) + (both[:, 256:384] + both[:, 384:512])

    features(x)

    second_axis(2)
    across(1)
    across(3)
    across(2)

    features(m4(x + 1))

    features(m4(x + 3))
    features(m4(x + 2))

    line = jnp.sum(lg[...], axis=0, keepdims=True)
    own_x = 2 * x + core
    for j in range(model // 128):
        g_x[own_x, j : j + 1, :] = line[:, 128 * j : 128 * (j + 1)]
    x_peers = [(k, dc) for k in range(NX) for dc in range(2) if k or dc]

    def x_dev(k, dc):
        return dev(m4(x + k), y, z, core + dc * (1 - 2 * core))

    for k, dc in x_peers:
        go(g_x.at[own_x], g_x.at[own_x], S_GX, gx, x_dev(k, dc))

    got(r1, rs1, to_right)
    for i in range(NY):
        dx, dy = xy(f, i)
        for dz in range(NZH):
            u[i, dz] = (t_keep[dx, 2 * dy + dz] + r1[0, i, dz].astype(F32)) + (
                r1[1, i, dz].astype(F32) + r1[2, i, dz].astype(F32)
            )
    for k in (1, 3, 2):
        go(u.at[m4(s + k)], u_recv.at[3 - k], S_RS2, rs2, dev_fs(f, m4(s + k)))

    got(g_x.at[pl.ds(0, 7)], gx, partner)
    g_y[y] = ((g_x[0] + g_x[1]) + (g_x[2] + g_x[3])) + ((g_x[4] + g_x[5]) + (g_x[6] + g_x[7]))
    for k in range(1, NY):
        go(g_y.at[y], g_y.at[y], S_GY, gy, dev(x, m4(y + k), z, core))

    got(u_recv, rs2, to_s_left)
    for dz in range(NZH):
        v[dz] = (u[s, dz] + u_recv[0, dz]) + (u_recv[1, dz] + u_recv[2, dz])

    lane = lax.broadcasted_iota(jnp.int32, (24, 128), 1)
    z_there = []
    for dz in range(NZH):
        for pair in range(2):
            top = v[dz, 0:24, 128 * pair : 128 * (pair + 1)]
            low = v[dz, 24:48, 128 * pair : 128 * (pair + 1)]
            z_send[4 * dz + 2 * pair] = jnp.where(lane < 64, top, pltpu.roll(low, 64, 1))
            z_send[4 * dz + 2 * pair + 1] = jnp.where(lane < 64, pltpu.roll(top, 64, 1), low)
            z_there += [NZL * dz + half_keep + 2 * pair, NZL * dz + half_keep + 2 * pair + 1]
    z_slot = lax.div(z, 2)
    for i in (7, 0, 6, 1, 5, 2, 4, 3):
        @pl.when(z_there[i] != z)
        def _():
            go(z_send.at[i], z_recv.at[z_slot], S_ZT, zsem, dev(x, y, z_there[i], core))

        @pl.when(z_there[i] == z)
        def _():
            z_recv[z_slot] = z_send[i]

    def inputs(i):
        @pl.loop(0, quarter // 64)
        def _(j):
            block = pl.ds(pl.multiple_of(i * quarter + j * 64, 64), 64)
            r = inv[block, :][:, :1]
            mean = jnp.sum(row_sum[block, :], axis=1, keepdims=True) * (1.0 / model)
            normed = act[block, :].astype(F32) * r
            out[block, :] = (r * (gain[...] * gs[block, :] - normed * mean)).astype(BF16)

    inputs(0)
    inputs(1)

    got(g_y.at[pl.ds(0, 3)], gy, partner)
    for pair in range(NZL // 2):
        row = pl.ds(4 * x + pair, 1)
        value = (g_y[0, row] + g_y[1, row]) + (g_y[2, row] + g_y[3, row])
        for dz in range(NZH):
            gz_send[dz * NZL + 2 * pair] = value
            gz_send[dz * NZL + 2 * pair + 1] = value
    for k in Z_ORDER:
        there = lax.rem(z + k, NZ)
        go(gz_send.at[there], gz_recv.at[z], S_GZ, gz, dev(x, y, there, core))
    gz_recv[z] = gz_send[z]

    inputs(2)
    inputs(3)

    @pl.when(to_self)
    def _():
        got(z_recv.at[pl.ds(0, 7)], zsem, partner)

    @pl.when(jnp.logical_not(to_self))
    def _():
        got(z_recv, zsem, partner)

    total = z_recv[0]
    for k in range(1, 8):
        total = total + z_recv[k]
    tail[0:24] = total * (1.0 / 16)

    got(gz_recv.at[pl.ds(0, NZ - 1)], gz, partner)
    total = gz_recv[0]
    for k in range(1, NZ):
        total = total + gz_recv[k]
    total = jnp.broadcast_to(total * (1.0 / 16), (8, 128))
    tail[24:32] = jnp.where(lax.rem(zl, 2) == 1, pltpu.roll(total, 64, 1), total)

    @pl.when(mine)
    def _():
        left_here(w.at[0, pl.ds(0, 7), 0], S_Z)

    left_here(p_send, S_P)
    left_here(w.at[pl.ds(0, 3), pl.ds(0, 5)], S_W)
    left_here(w.at[:, pl.ds(0, 4)], S_PASS)
    left_here(p.at[pl.ds(0, 3)], S_RS1)
    left_here(give, S_ZP)
    left_here(u.at[pl.ds(0, 3)], S_RS2)

    @pl.when(to_self)
    def _():
        left_here(z_send.at[pl.ds(0, 7)], S_ZT)

    @pl.when(jnp.logical_not(to_self))
    def _():
        left_here(z_send, S_ZT)

    left_here(g_x.at[pl.ds(0, 7)], S_GX)
    left_here(g_y.at[pl.ds(0, 3)], S_GY)
    left_here(gz_send.at[pl.ds(0, NZ - 1)], S_GZ)


def finish(raw, tail, out, weight_grads, gain_grads, buf, come, leave):
    away = pltpu.make_async_copy(raw, out, leave)
    away.start()
    into = pltpu.make_async_copy(tail, buf, come)
    into.start()
    into.wait()
    weight_grads[0:24] = buf[0:24, 0:64]
    weight_grads[24:48] = buf[0:24, 64:128]
    gain_grads[...] = buf[24:25, 0:64]
    away.wait()


def local(activations, norm_gain, key_weight, key_grads):
    tokens, model = activations.shape
    key = key_grads.shape[1]
    dma = pltpu.SemaphoreType.DMA
    scratch = [
        pltpu.VMEM((tokens, model), BF16),
        pltpu.VMEM((1, model), F32),
        pltpu.VMEM((tokens, key), BF16),
        pltpu.VMEM((tokens, model), F32),
        pltpu.VMEM((tokens, 128), F32),
        pltpu.VMEM((tokens, model), BF16),
        pltpu.VMEM((tokens, 128), F32),
        pltpu.VMEM((16, 48, tokens), BF16),
        pltpu.VMEM((NX, NZL, 4, 16, key), BF16),
        pltpu.VMEM((NX, 8, 48, 256), F32),
        pltpu.VMEM((NX, 8, 48, 256), F32),
        pltpu.VMEM((2, NX, 8, 48, 256), BF16),
        pltpu.VMEM((2, NX, 8, 48, 256), BF16),
        pltpu.VMEM((NX, 8, 48, 256), BF16),
        pltpu.VMEM((NX, 8, 48, 256), BF16),
        pltpu.VMEM((4, 4, NZH, 48, 256), BF16),
        pltpu.VMEM((3, 4, NZH, 48, 256), BF16),
        pltpu.VMEM((4, NZH, 48, 256), F32),
        pltpu.VMEM((3, NZH, 48, 256), F32),
        pltpu.VMEM((NZH, 48, 256), F32),
        pltpu.VMEM((8, 24, 128), F32),
        pltpu.VMEM((8, 24, 128), F32),
        pltpu.VMEM((8, model), F32),
        pltpu.VMEM((2 * NX, 16, 128), F32),
        pltpu.VMEM((NY, 16, 128), F32),
        pltpu.VMEM((NZ, 1, 128), F32),
        pltpu.VMEM((NZ, 1, 128), F32),
        dma((7,)),
        dma((11,)),
        dma((4,)),
        dma((4,)), dma((4,)), dma((4,)), dma((4,)), dma((4,)),
        dma((NX,)),
        dma((2 * NX,)),
        dma((2 * NX,)),
        dma,
        dma,
        dma,
        dma,
        dma,
        dma,
    ]
    vmem = pl.BlockSpec(memory_space=pltpu.VMEM)
    hbm = pl.BlockSpec(memory_space=pl.ANY)
    raw, tail = pl.pallas_call(
        kernel,
        out_shape=(
            pltpu.VMEM((tokens, model), BF16),
            pltpu.VMEM((32, 128), F32),
        ),
        in_specs=[hbm] * 4,
        out_specs=(vmem, vmem),
        scratch_shapes=scratch,
        compiler_params=pltpu.CompilerParams(
            collective_id=0, has_side_effects=True, vmem_limit_bytes=64900000
        ),
    )(activations, norm_gain.reshape(1, model), key_weight.reshape(4, 16, key), key_grads)
    input_grads, weight_grads, gain_grads = pl.pallas_call(
        finish,
        out_shape=(
            jax.ShapeDtypeStruct((tokens, model), BF16),
            jax.ShapeDtypeStruct((48, 64), F32),
            jax.ShapeDtypeStruct((1, 64), F32),
        ),
        in_specs=[hbm, hbm],
        out_specs=(hbm, vmem, vmem),
        scratch_shapes=[pltpu.VMEM((32, 128), F32), dma, dma],
        compiler_params=pltpu.CompilerParams(vmem_limit_bytes=1024 * 1024),
    )(raw, tail)
    return input_grads, weight_grads.T, gain_grads[0]


def solution(mesh):
    return jax.shard_map(
        local,
        mesh=mesh,
        in_specs=(P(("grp", "sub"), None), P(), P("sub", None), P(("grp", "sub"), None)),
        out_specs=(P(("grp", "sub"), None), P("sub", "grp"), P("sub")),
        check_vma=False,
    )
```

```python
import functools

import jax
import jax.numpy as jnp
from jax import lax
from jax.experimental import pallas as pl
from jax.experimental.pallas import tpu as pltpu
from jax.sharding import PartitionSpec as P

MESH = pl.DeviceIdType.MESH
F32 = jnp.float32
BF16 = jnp.bfloat16
NX, NY, NZL, NZH = 4, 4, 8, 2
NZ = NZL * NZH
Z_ORDER = (8, 7, 9, 6, 10, 5, 11, 4, 12, 3, 13, 2, 14, 1, 15)
S_Z, S_P, S_W, S_PASS, S_ZP, S_RS1, S_RS2, S_ZT, S_GX, S_GZ = range(10)


def kernel(
    act_hbm, gain_hbm, weight, grads_hbm,
    out, tail,
    act, gain, grads, gs, row_sum, scaled, inv, grads_t, w, both, t_give, t_keep, p_send, p_recv, give, given, p, r1, u, u_recv,
    v, z_send, z_recv, lg, g_send, g_recv, gz_send, gz_recv,
    load, send, agz, ag1, ag2l, ag2r, agf, agp, rsp, rsz, rs1, rs2, zsem, gx, gz, far_sem,
):
    g_idx, s_idx = lax.axis_index("grp"), lax.axis_index("sub")
    core = lax.rem(g_idx, 2)
    zh = lax.rem(lax.div(g_idx, 2), 2)
    y = lax.div(g_idx, 4)
    x = lax.div(s_idx, NZL)
    zl = lax.rem(s_idx, NZL)
    z = zh * NZL + zl
    f = x + core * (y - x)
    s = y + core * (x - y)
    tokens, model = act.shape
    key = grads.shape[1]

    def dev(dx, dy, dz, dc):
        return ((dy * 2 + lax.div(dz, NZL)) * 2 + dc, dx * NZL + lax.rem(dz, NZL))

    def xy(df, ds):
        return df + core * (ds - df), ds + core * (df - ds)

    def dev_fs(df, ds):
        dx, dy = xy(df, ds)
        return dev(dx, dy, z, core)

    def m4(a):
        return lax.rem(a, 4)

    partner = dev(x, y, z, 1 - core)
    right, left = m4(f + 1), m4(f + 3)
    s_right, s_left = m4(s + 1), m4(s + 3)

    def go(src, dst, group, recv, device):
        pltpu.make_async_remote_copy(
            src_ref=src, dst_ref=dst, send_sem=send.at[group], recv_sem=recv,
            device_id=device, device_id_type=MESH,
        ).start()

    def left_here(ref, group):
        pltpu.make_async_remote_copy(
            src_ref=ref, dst_ref=ref, send_sem=send.at[group], recv_sem=send.at[group],
            device_id=partner, device_id_type=MESH,
        ).wait_send()

    def got(dst, recv, device):
        pltpu.make_async_remote_copy(
            src_ref=dst, dst_ref=dst, send_sem=send.at[0], recv_sem=recv,
            device_id=device, device_id_type=MESH,
        ).wait_recv()

    barrier = pltpu.get_barrier_semaphore()
    peers = [partner]
    plane = [(dx, dy, dc) for dx in range(NX) for dy in (2, 1, 3, 0) for dc in range(2)]
    plane.remove((0, 0, 0))

    def plane_dev(dx, dy, dc):
        return dev(m4(x + dx), m4(y + dy), z, core + dc * (1 - 2 * core))

    peers += [plane_dev(*away) for away in plane if away != (0, 0, 1)]
    peers += [dev(x, y, lax.rem(z + k, NZ), core) for k in (1, 2, 3, 4, 12, 13, 14, 15)]
    for peer in peers:
        pl.semaphore_signal(barrier, inc=1, device_id=peer, device_id_type=MESH)

    quarter = tokens // 4
    loads = [
        pltpu.make_async_copy(
            act_hbm.at[pl.ds(i * quarter, quarter)], act.at[pl.ds(i * quarter, quarter)], load.at[i]
        )
        for i in range(4)
    ]
    loads.append(pltpu.make_async_copy(gain_hbm, gain, load.at[4]))
    loads.append(pltpu.make_async_copy(grads_hbm, grads, load.at[5]))
    for i in (4, 0, 1, 2, 3, 5):
        loads[i].start()

    rows = 64
    loads[4].wait()

    @pl.loop(0, tokens // rows)
    def _(i):
        @pl.when(lax.rem(i, 2) == 0)
        def _():
            at = pl.ds(pl.multiple_of(lax.div(i, 2) * quarter, quarter), quarter)
            pltpu.make_async_copy(act_hbm.at[at], act.at[at], load.at[lax.div(i, 2)]).wait()

        block = pl.ds(pl.multiple_of(i * rows, rows), rows)
        a = act[block, :].astype(F32)
        r = lax.rsqrt(jnp.sum(a * a, axis=1, keepdims=True) * (1.0 / model) + 1e-05)
        inv[block, :] = jnp.broadcast_to(r, (rows, 128))
        scaled[block, :] = (a * r * gain[...]).astype(BF16)

    loads[5].wait()
    grads_t[...] = grads[...].T.reshape(16, 48, tokens)

    pl.semaphore_wait(barrier, len(peers))
    for k in (4, 12):
        pl.semaphore_signal(
            far_sem, inc=1, device_id=dev(x, y, lax.rem(z + k, NZ), core), device_id_type=MESH
        )

    half = 4 * core
    mine = lax.div(zl, 4) == core
    z_offsets = (4, 3, 13, 2, 14, 1, 15)

    own_rows = pltpu.make_async_copy(weight.at[y], w.at[x, zl, y], load.at[6])

    @pl.when(mine)
    def _():
        for off in z_offsets:
            to = dev(x, y, lax.rem(z + off, NZ), core)
            go(weight.at[y], w.at[x, zl, y], S_Z, agz.at[lax.rem(zl, 4)], to)
        own_rows.start()

    keep_half = lax.rem(z, 2)
    half_keep = 4 * keep_half
    to_self = lax.div(zl, 4) == keep_half
    up, down = dev(x, y, lax.rem(z + 1, NZ), core), dev(x, y, lax.rem(z + NZ - 1, NZ), core)

    def products(n, i, side, own):
        rhs = scaled[:, pl.ds(pl.multiple_of(i * 512 + side * 256, 256), 256)]
        both[...] = jnp.dot(
            grads_t[...].reshape(key, tokens), rhs, preferred_element_type=F32
        ).reshape(16, 48, 256)
        for j in range(8):
            p_send[n, i, j] = both[2 * j + 1 - core].astype(BF16)
        go(p_send.at[n, i], p_recv.at[n, i], S_P, rsp.at[NX * n + i], partner)
        for j in range(8):
            own[i, j] = both[2 * j + core]

    @pl.loop(0, NX)
    def _(i):
        products(0, i, 1 - keep_half, t_give)

    @pl.loop(0, NX)
    def _(i):
        got(p_recv.at[0, i], rsp.at[i], partner)
        for j in range(8):
            give[i, j] = (t_give[i, j] + p_recv[0, i, j].astype(F32)).astype(BF16)
        go(give.at[i, pl.ds(0, 4)], given.at[i, pl.ds(0, 4)], S_ZP, rsz.at[i], up)
        go(give.at[i, pl.ds(4, 4)], given.at[i, pl.ds(4, 4)], S_ZP, rsz.at[NX + i], down)

    @pl.loop(0, NX)
    def _(i):
        products(1, i, keep_half, t_keep)


    def piece(df, ds):
        dx, dy = xy(df, ds)
        return w.at[dx, pl.ds(half, 4), dy]

    def pass_on(k, ds):
        at = piece(m4(f + k), ds)
        go(at, at, S_PASS, agp.at[xy(m4(f + k), ds)[0]], partner)

    to_right, to_left = dev_fs(right, s), dev_fs(left, s)
    to_s_right, to_s_left = dev_fs(f, s_right), dev_fs(f, s_left)
    opposite = m4(s + 2)
    to_opposite = dev_fs(f, opposite)

    def spread(k):
        at = piece(m4(f + k), s)
        go(at, at, S_W, ag2l.at[k], to_s_right)
        go(at, at, S_W, ag2r.at[k], to_s_left)

    for i in range(4):
        @pl.when(half + i != zl)
        def _():
            got(w.at[x, half + i, y], agz.at[i], partner)

    @pl.when(mine)
    def _():
        own_rows.wait()

    own = piece(f, s)
    for k in (2, 1, 3):
        go(own, own, S_W, ag1.at[4 - k], dev_fs(m4(f + k), s))
    spread(0)
    pass_on(0, s)

    @pl.loop(0, NX)
    def _(i):
        got(p_recv.at[1, i], rsp.at[NX + i], partner)
        for j in range(8):
            t_keep[i, j] += p_recv[1, i, j].astype(F32)

    def chunk(i):
        got(given.at[i, pl.ds(0, 4)], rsz.at[i], down)
        got(given.at[i, pl.ds(4, 4)], rsz.at[NX + i], up)
        for dy in range(NY):
            df, ds = xy(i, dy)
            for dz in range(NZH):
                total = t_keep[i, 2 * dy + dz] + given[i, 2 * dy + dz].astype(F32)
                t_keep[i, 2 * dy + dz] = total
                p[df, ds, dz] = total.astype(BF16)

            @pl.when(df != f)
            def _():
                go(p.at[df, ds], r1.at[3 - m4(df - f + 4), ds], S_RS1, rs1, dev_fs(df, s))

    def first_axis(k):
        got(piece(m4(f + k), s), ag1.at[k], dev_fs(m4(f + k), s))
        spread(k)
        if k == 2:
            at = piece(m4(f + k), s)
            go(at, at, S_W, agf.at[k], to_opposite)
        pass_on(k, s)

    def second_axis(k):
        at = piece(m4(f + k), s_left)
        got(at, ag2l.at[k], to_s_left)
        if k in (0, 1):
            go(at, at, S_W, agf.at[k], to_s_right)
        pass_on(k, s_left)
        at = piece(m4(f + k), s_right)
        got(at, ag2r.at[k], to_s_right)
        if k == 3:
            go(at, at, S_W, agf.at[k], to_s_left)
        pass_on(k, s_right)

    def across(k):
        got(piece(m4(f + k), opposite), agf.at[k], to_opposite)
        pass_on(k, opposite)

    chunk(0)
    first_axis(1)
    first_axis(3)
    chunk(1)
    second_axis(0)
    first_axis(2)
    second_axis(1)
    second_axis(3)
    chunk(2)
    second_axis(2)
    chunk(3)
    across(0)

    far = pl.ds(4 - half, 4)
    rows2 = 256
    lg[...] = jnp.zeros_like(lg)
    row_sum[...] = jnp.zeros_like(row_sum)

    def features(dx):
        got(w.at[dx, far], agp.at[dx], partner)
        columns = pl.ds(pl.multiple_of(dx * 512, 512), 512)

        @pl.loop(0, tokens // rows2)
        def _(i):
            block = pl.ds(pl.multiple_of(i * rows2, rows2), rows2)
            grad = lax.dot_general(
                grads[block, :], w[dx].reshape(512, key), (((1,), (1,)), ((), ())),
                preferred_element_type=F32,
            )
            gs[block, columns] = grad
            prod = grad * (act[block, columns].astype(F32) * inv[block, :][:, :1])
            lg[:, columns] += jnp.sum(prod.reshape(rows2 // 8, 8, 512), axis=0)
            prod = prod * gain[:, columns]
            row_sum[block, :] += (prod[:, 0:128] + prod[:, 128:256]) + (prod[:, 256:384] + prod[:, 384:512])

    me = (x * NY + y) * 2 + core

    def block(k):
        there = m4(x + k)
        features(there)
        g_send[k] = jnp.sum(
            lg[:, pl.ds(pl.multiple_of(there * 512, 512), 512)], axis=0, keepdims=True
        )
        for away in plane:
            if away[0] == k:
                go(g_send.at[k], g_recv.at[me], S_GX, gx, plane_dev(*away))

    block(0)
    g_recv[me] = g_send[0]

    across(1)
    across(3)
    across(2)

    got(r1, rs1, to_right)
    for i in range(NY):
        dx, dy = xy(f, i)
        for dz in range(NZH):
            u[i, dz] = (t_keep[dx, 2 * dy + dz] + r1[0, i, dz].astype(F32)) + (
                r1[1, i, dz].astype(F32) + r1[2, i, dz].astype(F32)
            )
    for k in (1, 3, 2):
        go(u.at[m4(s + k)], u_recv.at[3 - k], S_RS2, rs2, dev_fs(f, m4(s + k)))


    block(2)
    block(1)
    block(3)

    got(u_recv, rs2, to_s_left)
    for dz in range(NZH):
        v[dz] = (u[s, dz] + u_recv[0, dz]) + (u_recv[1, dz] + u_recv[2, dz])

    lane = lax.broadcasted_iota(jnp.int32, (24, 128), 1)
    z_there = []
    for dz in range(NZH):
        for pair in range(2):
            top = v[dz, 0:24, 128 * pair : 128 * (pair + 1)]
            low = v[dz, 24:48, 128 * pair : 128 * (pair + 1)]
            z_send[4 * dz + 2 * pair] = jnp.where(lane < 64, top, pltpu.roll(low, 64, 1))
            z_send[4 * dz + 2 * pair + 1] = jnp.where(lane < 64, pltpu.roll(top, 64, 1), low)
            z_there += [NZL * dz + half_keep + 2 * pair, NZL * dz + half_keep + 2 * pair + 1]
    z_slot = lax.div(z, 2)
    pl.semaphore_wait(far_sem, 2)
    for i in (7, 0, 6, 1, 5, 2, 4, 3):
        @pl.when(z_there[i] != z)
        def _():
            go(z_send.at[i], z_recv.at[z_slot], S_ZT, zsem, dev(x, y, z_there[i], core))

        @pl.when(z_there[i] == z)
        def _():
            z_recv[z_slot] = z_send[i]

    def inputs(i):
        @pl.loop(0, quarter // 64)
        def _(j):
            block = pl.ds(pl.multiple_of(i * quarter + j * 64, 64), 64)
            r = inv[block, :][:, :1]
            mean = jnp.sum(row_sum[block, :], axis=1, keepdims=True) * (1.0 / model)
            normed = act[block, :].astype(F32) * r
            out[block, :] = (r * (gain[...] * gs[block, :] - normed * mean)).astype(BF16)

    got(g_recv.at[pl.ds(0, 31)], gx, partner)
    line = g_recv[0]
    for i in range(1, 32):
        line = line + g_recv[i]
    for pair in range(NZL // 2):
        value = line[:, 128 * pair : 128 * (pair + 1)]
        for dz in range(NZH):
            gz_send[dz * NZL + 2 * pair] = value
            gz_send[dz * NZL + 2 * pair + 1] = value
    for k in Z_ORDER:
        there = lax.rem(z + k, NZ)
        go(gz_send.at[there], gz_recv.at[z], S_GZ, gz, dev(x, y, there, core))
    gz_recv[z] = gz_send[z]

    inputs(0)
    inputs(1)
    inputs(2)
    inputs(3)

    @pl.when(to_self)
    def _():
        got(z_recv.at[pl.ds(0, 7)], zsem, partner)

    @pl.when(jnp.logical_not(to_self))
    def _():
        got(z_recv, zsem, partner)

    total = z_recv[0]
    for k in range(1, 8):
        total = total + z_recv[k]
    tail[0:24] = total * (1.0 / 16)

    got(gz_recv.at[pl.ds(0, NZ - 1)], gz, partner)
    total = gz_recv[0]
    for k in range(1, NZ):
        total = total + gz_recv[k]
    total = jnp.broadcast_to(total * (1.0 / 16), (8, 128))
    tail[24:32] = jnp.where(lax.rem(zl, 2) == 1, pltpu.roll(total, 64, 1), total)

    @pl.when(mine)
    def _():
        left_here(w.at[0, pl.ds(0, 7), 0], S_Z)

    left_here(p_send, S_P)
    left_here(w.at[pl.ds(0, 3), pl.ds(0, 5)], S_W)
    left_here(w.at[:, pl.ds(0, 4)], S_PASS)
    left_here(p.at[pl.ds(0, 3)], S_RS1)
    left_here(give, S_ZP)
    left_here(u.at[pl.ds(0, 3)], S_RS2)

    @pl.when(to_self)
    def _():
        left_here(z_send.at[pl.ds(0, 7)], S_ZT)

    @pl.when(jnp.logical_not(to_self))
    def _():
        left_here(z_send, S_ZT)

    left_here(g_recv.at[pl.ds(0, 31)], S_GX)
    left_here(gz_send.at[pl.ds(0, NZ - 1)], S_GZ)


def finish(raw, tail, out, weight_grads, gain_grads, buf, come, leave):
    away = pltpu.make_async_copy(raw, out, leave)
    away.start()
    into = pltpu.make_async_copy(tail, buf, come)
    into.start()
    into.wait()
    weight_grads[0:24] = buf[0:24, 0:64]
    weight_grads[24:48] = buf[0:24, 64:128]
    gain_grads[...] = buf[24:25, 0:64]
    away.wait()


def local(activations, norm_gain, key_weight, key_grads):
    tokens, model = activations.shape
    key = key_grads.shape[1]
    dma = pltpu.SemaphoreType.DMA
    scratch = [
        pltpu.VMEM((tokens, model), BF16),
        pltpu.VMEM((1, model), F32),
        pltpu.VMEM((tokens, key), BF16),
        pltpu.VMEM((tokens, model), F32),
        pltpu.VMEM((tokens, 128), F32),
        pltpu.VMEM((tokens, model), BF16),
        pltpu.VMEM((tokens, 128), F32),
        pltpu.VMEM((16, 48, tokens), BF16),
        pltpu.VMEM((NX, NZL, 4, 16, key), BF16),
        pltpu.VMEM((16, 48, 256), F32),
        pltpu.VMEM((NX, 8, 48, 256), F32),
        pltpu.VMEM((NX, 8, 48, 256), F32),
        pltpu.VMEM((2, NX, 8, 48, 256), BF16),
        pltpu.VMEM((2, NX, 8, 48, 256), BF16),
        pltpu.VMEM((NX, 8, 48, 256), BF16),
        pltpu.VMEM((NX, 8, 48, 256), BF16),
        pltpu.VMEM((4, 4, NZH, 48, 256), BF16),
        pltpu.VMEM((3, 4, NZH, 48, 256), BF16),
        pltpu.VMEM((4, NZH, 48, 256), F32),
        pltpu.VMEM((3, NZH, 48, 256), F32),
        pltpu.VMEM((NZH, 48, 256), F32),
        pltpu.VMEM((8, 24, 128), F32),
        pltpu.VMEM((8, 24, 128), F32),
        pltpu.VMEM((8, model), F32),
        pltpu.VMEM((NX, 1, 512), F32),
        pltpu.VMEM((32, 1, 512), F32),
        pltpu.VMEM((NZ, 1, 128), F32),
        pltpu.VMEM((NZ, 1, 128), F32),
        dma((7,)),
        dma((10,)),
        dma((4,)),
        dma((4,)), dma((4,)), dma((4,)), dma((4,)),
        dma((NX,)),
        dma((2 * NX,)),
        dma((2 * NX,)),
        dma,
        dma,
        dma,
        dma,
        dma,
        pltpu.SemaphoreType.REGULAR,
    ]
    vmem = pl.BlockSpec(memory_space=pltpu.VMEM)
    hbm = pl.BlockSpec(memory_space=pl.ANY)
    raw, tail = pl.pallas_call(
        kernel,
        out_shape=(
            pltpu.VMEM((tokens, model), BF16),
            pltpu.VMEM((32, 128), F32),
        ),
        in_specs=[hbm] * 4,
        out_specs=(vmem, vmem),
        scratch_shapes=scratch,
        compiler_params=pltpu.CompilerParams(
            collective_id=0, has_side_effects=True, vmem_limit_bytes=64900000
        ),
    )(activations, norm_gain.reshape(1, model), key_weight.reshape(4, 16, key), key_grads)
    input_grads, weight_grads, gain_grads = pl.pallas_call(
        finish,
        out_shape=(
            jax.ShapeDtypeStruct((tokens, model), BF16),
            jax.ShapeDtypeStruct((48, 64), F32),
            jax.ShapeDtypeStruct((1, 64), F32),
        ),
        in_specs=[hbm, hbm],
        out_specs=(hbm, vmem, vmem),
        scratch_shapes=[pltpu.VMEM((32, 128), F32), dma, dma],
        compiler_params=pltpu.CompilerParams(vmem_limit_bytes=1024 * 1024),
    )(raw, tail)
    return input_grads, weight_grads.T, gain_grads[0]


def solution(mesh):
    return jax.shard_map(
        local,
        mesh=mesh,
        in_specs=(P(("grp", "sub"), None), P(), P("sub", None), P(("grp", "sub"), None)),
        out_specs=(P(("grp", "sub"), None), P("sub", "grp"), P("sub")),
        check_vma=False,
    )
```

```python
import functools

import jax
import jax.numpy as jnp
from jax import lax
from jax.experimental import pallas as pl
from jax.experimental.pallas import tpu as pltpu
from jax.sharding import PartitionSpec as P

MESH = pl.DeviceIdType.MESH
F32 = jnp.float32
BF16 = jnp.bfloat16
NX, NY, NZL, NZH = 4, 4, 8, 2
NZ = NZL * NZH
Z_ORDER = (8, 7, 9, 6, 10, 5, 11, 4, 12, 3, 13, 2, 14, 1, 15)
S_Z, S_P, S_W, S_PASS, S_ZP, S_RS1, S_RS2, S_ZT, S_GX, S_GZ = range(10)


def kernel(
    act_hbm, gain_hbm, weight, grads_hbm,
    out, tail,
    act, gain, grads, gs, row_sum, scaled, inv, grads_t, w, both, t_give, t_keep, p_send, p_recv, give, given, p, r1, u, u_recv,
    v, z_send, z_recv, lg, g_send, g_recv, gz_send, gz_recv,
    load, send, agz, ag1, ag2, agzz, agp, rsp, rsz, rs1, rs2, zsem, gx, gz, far_sem,
):
    g_idx, s_idx = lax.axis_index("grp"), lax.axis_index("sub")
    core = lax.rem(g_idx, 2)
    zh = lax.rem(lax.div(g_idx, 2), 2)
    y = lax.div(g_idx, 4)
    x = lax.div(s_idx, NZL)
    zl = lax.rem(s_idx, NZL)
    z = zh * NZL + zl
    f = x + core * (y - x)
    s = y + core * (x - y)
    tokens, model = act.shape
    key = grads.shape[1]

    def dev(dx, dy, dz, dc):
        return ((dy * 2 + lax.div(dz, NZL)) * 2 + dc, dx * NZL + lax.rem(dz, NZL))

    def xy(df, ds):
        return df + core * (ds - df), ds + core * (df - ds)

    def dev_fs(df, ds):
        dx, dy = xy(df, ds)
        return dev(dx, dy, z, core)

    def m4(a):
        return lax.rem(a, 4)

    partner = dev(x, y, z, 1 - core)

    def go(src, dst, group, recv, device):
        pltpu.make_async_remote_copy(
            src_ref=src, dst_ref=dst, send_sem=send.at[group], recv_sem=recv,
            device_id=device, device_id_type=MESH,
        ).start()

    def left_here(ref, group):
        pltpu.make_async_remote_copy(
            src_ref=ref, dst_ref=ref, send_sem=send.at[group], recv_sem=send.at[group],
            device_id=partner, device_id_type=MESH,
        ).wait_send()

    def got(dst, recv, device):
        pltpu.make_async_remote_copy(
            src_ref=dst, dst_ref=dst, send_sem=send.at[0], recv_sem=recv,
            device_id=device, device_id_type=MESH,
        ).wait_recv()

    barrier = pltpu.get_barrier_semaphore()
    peers = [partner]
    plane = [(dx, dy, dc) for dx in range(NX) for dy in (2, 1, 3, 0) for dc in range(2)]
    plane.remove((0, 0, 0))

    def plane_dev(dx, dy, dc):
        return dev(m4(x + dx), m4(y + dy), z, core + dc * (1 - 2 * core))

    peers += [plane_dev(*away) for away in plane if away != (0, 0, 1)]
    peers += [dev(x, y, lax.rem(z + k, NZ), core) for k in (1, 2, 3, 4, 12, 13, 14, 15)]
    for peer in peers:
        pl.semaphore_signal(barrier, inc=1, device_id=peer, device_id_type=MESH)

    quarter = tokens // 4
    loads = [
        pltpu.make_async_copy(
            act_hbm.at[pl.ds(i * quarter, quarter)], act.at[pl.ds(i * quarter, quarter)], load.at[i]
        )
        for i in range(4)
    ]
    loads.append(pltpu.make_async_copy(gain_hbm, gain, load.at[4]))
    loads.append(pltpu.make_async_copy(grads_hbm, grads, load.at[5]))
    for i in (4, 0, 1, 2, 3, 5):
        loads[i].start()

    rows = 64
    loads[4].wait()

    @pl.loop(0, tokens // rows)
    def _(i):
        @pl.when(lax.rem(i, 2) == 0)
        def _():
            at = pl.ds(pl.multiple_of(lax.div(i, 2) * quarter, quarter), quarter)
            pltpu.make_async_copy(act_hbm.at[at], act.at[at], load.at[lax.div(i, 2)]).wait()

        block = pl.ds(pl.multiple_of(i * rows, rows), rows)
        a = act[block, :].astype(F32)
        r = lax.rsqrt(jnp.sum(a * a, axis=1, keepdims=True) * (1.0 / model) + 1e-05)
        inv[block, :] = jnp.broadcast_to(r, (rows, 128))
        scaled[block, :] = (a * r * gain[...]).astype(BF16)

    loads[5].wait()
    grads_t[...] = grads[...].T.reshape(16, 48, tokens)

    pl.semaphore_wait(barrier, len(peers))
    for k in (4, 12):
        pl.semaphore_signal(
            far_sem, inc=1, device_id=dev(x, y, lax.rem(z + k, NZ), core), device_id_type=MESH
        )

    half = 4 * core
    mine = lax.div(zl, 4) == core
    z_offsets = (4, 3, 13, 2, 14, 1, 15)

    own_rows = pltpu.make_async_copy(weight.at[y], w.at[x, zl, y], load.at[6])

    @pl.when(mine)
    def _():
        for off in z_offsets:
            to = dev(x, y, lax.rem(z + off, NZ), core)
            go(weight.at[y], w.at[x, zl, y], S_Z, agz.at[lax.rem(zl, 4)], to)
        own_rows.start()

    keep_half = lax.rem(z, 2)
    half_keep = 4 * keep_half
    to_self = lax.div(zl, 4) == keep_half
    up, down = dev(x, y, lax.rem(z + 1, NZ), core), dev(x, y, lax.rem(z + NZ - 1, NZ), core)

    def products(n, i, side, own):
        rhs = scaled[:, pl.ds(pl.multiple_of(i * 512 + side * 256, 256), 256)]
        both[...] = jnp.dot(
            grads_t[...].reshape(key, tokens), rhs, preferred_element_type=F32
        ).reshape(16, 48, 256)
        for j in range(8):
            p_send[n, i, j] = both[2 * j + 1 - core].astype(BF16)
        go(p_send.at[n, i], p_recv.at[n, i], S_P, rsp.at[NX * n + i], partner)
        for j in range(8):
            own[i, j] = both[2 * j + core]

    @pl.loop(0, NX)
    def _(i):
        products(0, i, 1 - keep_half, t_give)

    @pl.loop(0, NX)
    def _(i):
        got(p_recv.at[0, i], rsp.at[i], partner)
        for j in range(8):
            give[i, j] = (t_give[i, j] + p_recv[0, i, j].astype(F32)).astype(BF16)
        go(give.at[i, pl.ds(0, 4)], given.at[i, pl.ds(0, 4)], S_ZP, rsz.at[i], up)
        go(give.at[i, pl.ds(4, 4)], given.at[i, pl.ds(4, 4)], S_ZP, rsz.at[NX + i], down)

    @pl.loop(0, NX)
    def _(i):
        products(1, i, keep_half, t_keep)


    side = (1 + 2 * keep_half, 3 - 2 * keep_half)

    def piece(n, m, other=0):
        k = (0, side[other], 2)[n]
        dx, dy = xy(m4(f + k), m4(s + m))
        if n < 2:
            return w.at[dx, pl.ds(half, 4), dy], dx
        return w.at[dx, pl.ds(half + 2 * (keep_half + other * (1 - 2 * keep_half)), 2), dy], dx

    def pass_on(n, m, other=0):
        at, dx = piece(n, m, other)
        go(at, at, S_PASS, agp.at[dx], partner)

    s_devs = [dev_fs(f, m4(s + m)) for m in range(4)]

    def spread(n):
        at, _ = piece(n, 0)
        go(at, at, S_W, ag2.at[4 * n + 3], s_devs[1])
        go(at, at, S_W, ag2.at[4 * n + 1], s_devs[3])

    def along_z(n, m):
        if n:
            at, _ = piece(n, m)
            go(at, at, S_W, agzz.at[4 * (n - 1) + m], up if n == 1 and m != 2 else down)

    for i in range(4):
        @pl.when(half + i != zl)
        def _():
            got(w.at[x, half + i, y], agz.at[i], partner)

    @pl.when(mine)
    def _():
        own_rows.wait()

    dx, dy = xy(f, s)
    own_half = w.at[dx, pl.ds(half + 2 * keep_half, 2), dy]
    go(own_half, own_half, S_W, ag1.at[1], dev_fs(m4(f + 2), s))
    own, _ = piece(0, 0)
    go(own, own, S_W, ag1.at[0], dev_fs(m4(f + 3 + 2 * keep_half), s))
    spread(0)
    pass_on(0, 0)

    @pl.loop(0, NX)
    def _(i):
        got(p_recv.at[1, i], rsp.at[NX + i], partner)
        for j in range(8):
            t_keep[i, j] += p_recv[1, i, j].astype(F32)

    def chunk(i):
        got(given.at[i, pl.ds(0, 4)], rsz.at[i], down)
        got(given.at[i, pl.ds(4, 4)], rsz.at[NX + i], up)
        for dy in range(NY):
            df, ds = xy(i, dy)
            for dz in range(NZH):
                total = t_keep[i, 2 * dy + dz] + given[i, 2 * dy + dz].astype(F32)
                t_keep[i, 2 * dy + dz] = total
                p[df, ds, dz] = total.astype(BF16)

            @pl.when(df != f)
            def _():
                go(p.at[df, ds], r1.at[3 - m4(df - f + 4), ds], S_RS1, rs1, dev_fs(df, s))

    chunk(0)
    for n in (1, 2):
        got(piece(n, 0)[0], ag1.at[n - 1], partner)
        spread(n)
        along_z(n, 0)
        pass_on(n, 0)

    def beside(n, m):
        at, _ = piece(n, m)
        got(at, ag2.at[4 * n + m], s_devs[m])
        if m == (3, 1, 3)[n]:
            go(at, at, S_W, ag2.at[4 * n + 2], s_devs[4 - m])
        along_z(n, m)
        pass_on(n, m)

    chunk(1)
    beside(0, 3)
    beside(0, 1)
    chunk(2)
    beside(1, 1)
    beside(1, 3)
    beside(2, 3)
    beside(2, 1)
    chunk(3)
    beside(0, 2)
    beside(1, 2)
    beside(2, 2)

    def from_z(n, m):
        got(piece(n, m, 1)[0], agzz.at[4 * (n - 1) + m], down if n == 1 and m != 2 else up)
        pass_on(n, m, 1)

    for m in (0, 3, 1):
        from_z(1, m)
        from_z(2, m)

    far = pl.ds(4 - half, 4)
    rows2 = 256
    lg[...] = jnp.zeros_like(lg)
    row_sum[...] = jnp.zeros_like(row_sum)

    def features(dx):
        got(w.at[dx, far], agp.at[dx], partner)
        columns = pl.ds(pl.multiple_of(dx * 512, 512), 512)

        @pl.loop(0, tokens // rows2)
        def _(i):
            block = pl.ds(pl.multiple_of(i * rows2, rows2), rows2)
            grad = lax.dot_general(
                grads[block, :], w[dx].reshape(512, key), (((1,), (1,)), ((), ())),
                preferred_element_type=F32,
            )
            gs[block, columns] = grad
            prod = grad * (act[block, columns].astype(F32) * inv[block, :][:, :1])
            lg[:, columns] += jnp.sum(prod.reshape(rows2 // 8, 8, 512), axis=0)
            prod = prod * gain[:, columns]
            row_sum[block, :] += (prod[:, 0:128] + prod[:, 128:256]) + (prod[:, 256:384] + prod[:, 384:512])

    me = (x * NY + y) * 2 + core

    def block(k):
        there = m4(x + k)
        features(there)
        g_send[k] = jnp.sum(
            lg[:, pl.ds(pl.multiple_of(there * 512, 512), 512)], axis=0, keepdims=True
        )
        for away in plane:
            if away[0] == k:
                go(g_send.at[k], g_recv.at[me], S_GX, gx, plane_dev(*away))

    block(0)
    g_recv[me] = g_send[0]

    from_z(1, 2)
    from_z(2, 2)

    got(r1, rs1, partner)
    for i in range(NY):
        dx, dy = xy(f, i)
        for dz in range(NZH):
            u[i, dz] = (t_keep[dx, 2 * dy + dz] + r1[0, i, dz].astype(F32)) + (
                r1[1, i, dz].astype(F32) + r1[2, i, dz].astype(F32)
            )
    for k in (1, 3, 2):
        go(u.at[m4(s + k)], u_recv.at[3 - k], S_RS2, rs2, dev_fs(f, m4(s + k)))

    block(2)
    block(1)
    block(3)

    got(u_recv, rs2, partner)
    for dz in range(NZH):
        v[dz] = (u[s, dz] + u_recv[0, dz]) + (u_recv[1, dz] + u_recv[2, dz])

    lane = lax.broadcasted_iota(jnp.int32, (24, 128), 1)
    z_there = []
    for dz in range(NZH):
        for pair in range(2):
            top = v[dz, 0:24, 128 * pair : 128 * (pair + 1)]
            low = v[dz, 24:48, 128 * pair : 128 * (pair + 1)]
            z_send[4 * dz + 2 * pair] = jnp.where(lane < 64, top, pltpu.roll(low, 64, 1))
            z_send[4 * dz + 2 * pair + 1] = jnp.where(lane < 64, pltpu.roll(top, 64, 1), low)
            z_there += [NZL * dz + half_keep + 2 * pair, NZL * dz + half_keep + 2 * pair + 1]
    z_slot = lax.div(z, 2)
    pl.semaphore_wait(far_sem, 2)
    for i in (7, 0, 6, 1, 5, 2, 4, 3):
        @pl.when(z_there[i] != z)
        def _():
            go(z_send.at[i], z_recv.at[z_slot], S_ZT, zsem, dev(x, y, z_there[i], core))

        @pl.when(z_there[i] == z)
        def _():
            z_recv[z_slot] = z_send[i]

    def inputs(i):
        @pl.loop(0, quarter // 64)
        def _(j):
            block = pl.ds(pl.multiple_of(i * quarter + j * 64, 64), 64)
            r = inv[block, :][:, :1]
            mean = jnp.sum(row_sum[block, :], axis=1, keepdims=True) * (1.0 / model)
            normed = act[block, :].astype(F32) * r
            out[block, :] = (r * (gain[...] * gs[block, :] - normed * mean)).astype(BF16)

    got(g_recv.at[pl.ds(0, 31)], gx, partner)
    line = g_recv[0]
    for i in range(1, 32):
        line = line + g_recv[i]
    for pair in range(NZL // 2):
        value = line[:, 128 * pair : 128 * (pair + 1)]
        for dz in range(NZH):
            gz_send[dz * NZL + 2 * pair] = value
            gz_send[dz * NZL + 2 * pair + 1] = value
    for k in Z_ORDER:
        there = lax.rem(z + k, NZ)
        go(gz_send.at[there], gz_recv.at[z], S_GZ, gz, dev(x, y, there, core))
    gz_recv[z] = gz_send[z]

    inputs(0)
    inputs(1)
    inputs(2)
    inputs(3)

    @pl.when(to_self)
    def _():
        got(z_recv.at[pl.ds(0, 7)], zsem, partner)

    @pl.when(jnp.logical_not(to_self))
    def _():
        got(z_recv, zsem, partner)

    total = z_recv[0]
    for k in range(1, 8):
        total = total + z_recv[k]
    tail[0:24] = total * (1.0 / 16)

    got(gz_recv.at[pl.ds(0, NZ - 1)], gz, partner)
    total = gz_recv[0]
    for k in range(1, NZ):
        total = total + gz_recv[k]
    total = jnp.broadcast_to(total * (1.0 / 16), (8, 128))
    tail[24:32] = jnp.where(lax.rem(zl, 2) == 1, pltpu.roll(total, 64, 1), total)

    @pl.when(mine)
    def _():
        left_here(w.at[0, pl.ds(0, 7), 0], S_Z)

    left_here(p_send, S_P)
    left_here(w.at[pl.ds(0, 3), pl.ds(0, 5)], S_W)
    left_here(w.at[:, pl.ds(0, 4)], S_PASS)
    left_here(p.at[pl.ds(0, 3)], S_RS1)
    left_here(give, S_ZP)
    left_here(u.at[pl.ds(0, 3)], S_RS2)

    @pl.when(to_self)
    def _():
        left_here(z_send.at[pl.ds(0, 7)], S_ZT)

    @pl.when(jnp.logical_not(to_self))
    def _():
        left_here(z_send, S_ZT)

    left_here(g_recv.at[pl.ds(0, 31)], S_GX)
    left_here(gz_send.at[pl.ds(0, NZ - 1)], S_GZ)


def finish(raw, tail, out, weight_grads, gain_grads, buf, come, leave):
    away = pltpu.make_async_copy(raw, out, leave)
    away.start()
    into = pltpu.make_async_copy(tail, buf, come)
    into.start()
    into.wait()
    weight_grads[0:24] = buf[0:24, 0:64]
    weight_grads[24:48] = buf[0:24, 64:128]
    gain_grads[...] = buf[24:25, 0:64]
    away.wait()


def local(activations, norm_gain, key_weight, key_grads):
    tokens, model = activations.shape
    key = key_grads.shape[1]
    dma = pltpu.SemaphoreType.DMA
    scratch = [
        pltpu.VMEM((tokens, model), BF16),
        pltpu.VMEM((1, model), F32),
        pltpu.VMEM((tokens, key), BF16),
        pltpu.VMEM((tokens, model), F32),
        pltpu.VMEM((tokens, 128), F32),
        pltpu.VMEM((tokens, model), BF16),
        pltpu.VMEM((tokens, 128), F32),
        pltpu.VMEM((16, 48, tokens), BF16),
        pltpu.VMEM((NX, NZL, 4, 16, key), BF16),
        pltpu.VMEM((16, 48, 256), F32),
        pltpu.VMEM((NX, 8, 48, 256), F32),
        pltpu.VMEM((NX, 8, 48, 256), F32),
        pltpu.VMEM((2, NX, 8, 48, 256), BF16),
        pltpu.VMEM((2, NX, 8, 48, 256), BF16),
        pltpu.VMEM((NX, 8, 48, 256), BF16),
        pltpu.VMEM((NX, 8, 48, 256), BF16),
        pltpu.VMEM((4, 4, NZH, 48, 256), BF16),
        pltpu.VMEM((3, 4, NZH, 48, 256), BF16),
        pltpu.VMEM((4, NZH, 48, 256), F32),
        pltpu.VMEM((3, NZH, 48, 256), F32),
        pltpu.VMEM((NZH, 48, 256), F32),
        pltpu.VMEM((8, 24, 128), F32),
        pltpu.VMEM((8, 24, 128), F32),
        pltpu.VMEM((8, model), F32),
        pltpu.VMEM((NX, 1, 512), F32),
        pltpu.VMEM((32, 1, 512), F32),
        pltpu.VMEM((NZ, 1, 128), F32),
        pltpu.VMEM((NZ, 1, 128), F32),
        dma((7,)),
        dma((10,)),
        dma((4,)),
        dma((2,)),
        dma((12,)),
        dma((8,)),
        dma((NX,)),
        dma((2 * NX,)),
        dma((2 * NX,)),
        dma,
        dma,
        dma,
        dma,
        dma,
        pltpu.SemaphoreType.REGULAR,
    ]
    vmem = pl.BlockSpec(memory_space=pltpu.VMEM)
    hbm = pl.BlockSpec(memory_space=pl.ANY)
    raw, tail = pl.pallas_call(
        kernel,
        out_shape=(
            pltpu.VMEM((tokens, model), BF16),
            pltpu.VMEM((32, 128), F32),
        ),
        in_specs=[hbm] * 4,
        out_specs=(vmem, vmem),
        scratch_shapes=scratch,
        compiler_params=pltpu.CompilerParams(
            collective_id=0, has_side_effects=True, vmem_limit_bytes=64900000
        ),
    )(activations, norm_gain.reshape(1, model), key_weight.reshape(4, 16, key), key_grads)
    input_grads, weight_grads, gain_grads = pl.pallas_call(
        finish,
        out_shape=(
            jax.ShapeDtypeStruct((tokens, model), BF16),
            jax.ShapeDtypeStruct((48, 64), F32),
            jax.ShapeDtypeStruct((1, 64), F32),
        ),
        in_specs=[hbm, hbm],
        out_specs=(hbm, vmem, vmem),
        scratch_shapes=[pltpu.VMEM((32, 128), F32), dma, dma],
        compiler_params=pltpu.CompilerParams(vmem_limit_bytes=1024 * 1024),
    )(raw, tail)
    return input_grads, weight_grads.T, gain_grads[0]


def solution(mesh):
    return jax.shard_map(
        local,
        mesh=mesh,
        in_specs=(P(("grp", "sub"), None), P(), P("sub", None), P(("grp", "sub"), None)),
        out_specs=(P(("grp", "sub"), None), P("sub", "grp"), P("sub")),
        check_vma=False,
    )
```

```python
import functools

import jax
import jax.numpy as jnp
from jax import lax
from jax.experimental import pallas as pl
from jax.experimental.pallas import tpu as pltpu
from jax.sharding import PartitionSpec as P

MESH = pl.DeviceIdType.MESH
F32 = jnp.float32
BF16 = jnp.bfloat16
NX, NY, NZL, NZH = 4, 4, 8, 2
NZ = NZL * NZH
Z_ORDER = (8, 7, 9, 6, 10, 5, 11, 4, 12, 3, 13, 2, 14, 1, 15)
S_Z, S_P, S_W, S_PASS, S_ZP, S_RS1, S_RS2, S_ZT, S_GX, S_GZ = range(10)


def kernel(
    act_hbm, gain_hbm, weight, grads_hbm,
    out, tail,
    act, gain, grads, gs, row_sum, scaled, inv, grads_t, w, both, t_give, t_keep, p_send, p_recv, give, given, p, r1, u, u_recv,
    v, z_send, z_recv, lg, g_send, g_recv, gz_send, gz_recv,
    load, send, agz, ag1, ag2, agzz, agp, rsp, rsz, rs1, rs2, zsem, gx, gz, far_sem,
):
    g_idx, s_idx = lax.axis_index("grp"), lax.axis_index("sub")
    core = lax.rem(g_idx, 2)
    zh = lax.rem(lax.div(g_idx, 2), 2)
    y = lax.div(g_idx, 4)
    x = lax.div(s_idx, NZL)
    zl = lax.rem(s_idx, NZL)
    z = zh * NZL + zl
    f = x + core * (y - x)
    s = y + core * (x - y)
    tokens, model = act.shape
    key = grads.shape[1]

    def dev(dx, dy, dz, dc):
        return ((dy * 2 + lax.div(dz, NZL)) * 2 + dc, dx * NZL + lax.rem(dz, NZL))

    def xy(df, ds):
        return df + core * (ds - df), ds + core * (df - ds)

    def dev_fs(df, ds):
        dx, dy = xy(df, ds)
        return dev(dx, dy, z, core)

    def m4(a):
        return lax.rem(a, 4)

    partner = dev(x, y, z, 1 - core)

    def go(src, dst, group, recv, device):
        pltpu.make_async_remote_copy(
            src_ref=src, dst_ref=dst, send_sem=send.at[group], recv_sem=recv,
            device_id=device, device_id_type=MESH,
        ).start()

    def left_here(ref, group):
        pltpu.make_async_remote_copy(
            src_ref=ref, dst_ref=ref, send_sem=send.at[group], recv_sem=send.at[group],
            device_id=partner, device_id_type=MESH,
        ).wait_send()

    def got(dst, recv, device):
        pltpu.make_async_remote_copy(
            src_ref=dst, dst_ref=dst, send_sem=send.at[0], recv_sem=recv,
            device_id=device, device_id_type=MESH,
        ).wait_recv()

    barrier = pltpu.get_barrier_semaphore()
    peers = [partner]
    plane = [(dx, dy, dc) for dx in range(NX) for dy in (2, 1, 3, 0) for dc in range(2)]
    plane.remove((0, 0, 0))

    def plane_dev(dx, dy, dc):
        return dev(m4(x + dx), m4(y + dy), z, core + dc * (1 - 2 * core))

    peers += [plane_dev(*away) for away in plane if away != (0, 0, 1)]
    peers += [dev(x, y, lax.rem(z + k, NZ), core) for k in (1, 2, 3, 4, 12, 13, 14, 15)]
    for peer in peers:
        pl.semaphore_signal(barrier, inc=1, device_id=peer, device_id_type=MESH)

    quarter = tokens // 4
    loads = [
        pltpu.make_async_copy(
            act_hbm.at[pl.ds(i * quarter, quarter)], act.at[pl.ds(i * quarter, quarter)], load.at[i]
        )
        for i in range(4)
    ]
    loads.append(pltpu.make_async_copy(gain_hbm, gain, load.at[4]))
    loads.append(pltpu.make_async_copy(grads_hbm, grads, load.at[5]))
    for i in (4, 0, 1, 2, 3, 5):
        loads[i].start()

    rows = 64
    loads[4].wait()

    @pl.loop(0, tokens // rows)
    def _(i):
        @pl.when(lax.rem(i, 2) == 0)
        def _():
            at = pl.ds(pl.multiple_of(lax.div(i, 2) * quarter, quarter), quarter)
            pltpu.make_async_copy(act_hbm.at[at], act.at[at], load.at[lax.div(i, 2)]).wait()

        block = pl.ds(pl.multiple_of(i * rows, rows), rows)
        a = act[block, :].astype(F32)
        r = lax.rsqrt(jnp.sum(a * a, axis=1, keepdims=True) * (1.0 / model) + 1e-05)
        inv[block, :] = jnp.broadcast_to(r, (rows, 128))
        scaled[block, :] = (a * r * gain[...]).astype(BF16)

    loads[5].wait()
    grads_t[...] = grads[...].T.reshape(16, 48, tokens)

    pl.semaphore_wait(barrier, len(peers))
    for k in (4, 12):
        pl.semaphore_signal(
            far_sem, inc=1, device_id=dev(x, y, lax.rem(z + k, NZ), core), device_id_type=MESH
        )

    half = 4 * core
    mine = lax.div(zl, 4) == core
    z_offsets = (4, 3, 13, 2, 14, 1, 15)

    own_rows = pltpu.make_async_copy(weight.at[y], w.at[x, zl, y], load.at[6])

    @pl.when(mine)
    def _():
        for off in z_offsets:
            to = dev(x, y, lax.rem(z + off, NZ), core)
            go(weight.at[y], w.at[x, zl, y], S_Z, agz.at[lax.rem(zl, 4)], to)
        own_rows.start()

    keep_half = lax.rem(z, 2)
    half_keep = 4 * keep_half
    to_self = lax.div(zl, 4) == keep_half
    up, down = dev(x, y, lax.rem(z + 1, NZ), core), dev(x, y, lax.rem(z + NZ - 1, NZ), core)

    def products(n, i, side, own):
        rhs = scaled[:, pl.ds(pl.multiple_of(i * 512 + side * 256, 256), 256)]
        both[...] = jnp.dot(
            grads_t[...].reshape(key, tokens), rhs, preferred_element_type=F32
        ).reshape(16, 48, 256)
        for j in range(8):
            p_send[n, i, j] = both[2 * j + 1 - core].astype(BF16)
        go(p_send.at[n, i], p_recv.at[n, i], S_P, rsp.at[NX * n + i], partner)
        for j in range(8):
            own[i, j] = both[2 * j + core]

    @pl.loop(0, NX)
    def _(i):
        products(0, i, 1 - keep_half, t_give)

    @pl.loop(0, NX)
    def _(i):
        got(p_recv.at[0, i], rsp.at[i], partner)
        for j in range(8):
            give[i, j] = (t_give[i, j] + p_recv[0, i, j].astype(F32)).astype(BF16)
        go(give.at[i, pl.ds(0, 4)], given.at[i, pl.ds(0, 4)], S_ZP, rsz.at[i], up)
        go(give.at[i, pl.ds(4, 4)], given.at[i, pl.ds(4, 4)], S_ZP, rsz.at[NX + i], down)

    @pl.loop(0, NX)
    def _(i):
        products(1, i, keep_half, t_keep)


    side = (1 + 2 * keep_half, 3 - 2 * keep_half)

    def piece(n, m, other=0):
        k = (0, side[other], 2)[n]
        dx, dy = xy(m4(f + k), m4(s + m))
        if n < 2:
            return w.at[dx, pl.ds(half, 4), dy], dx
        return w.at[dx, pl.ds(half + 2 * (keep_half + other * (1 - 2 * keep_half)), 2), dy], dx

    def pass_on(n, m, other=0):
        at, dx = piece(n, m, other)
        go(at, at, S_PASS, agp.at[dx], partner)

    s_devs = [dev_fs(f, m4(s + m)) for m in range(4)]

    def spread(n):
        at, _ = piece(n, 0)
        go(at, at, S_W, ag2.at[4 * n + 3], s_devs[1])
        go(at, at, S_W, ag2.at[4 * n + 1], s_devs[3])

    def along_z(n, m):
        if n:
            at, _ = piece(n, m)
            go(at, at, S_W, agzz.at[4 * (n - 1) + m], up if n == 1 and m != 2 else down)

    for i in range(4):
        @pl.when(half + i != zl)
        def _():
            got(w.at[x, half + i, y], agz.at[i], partner)

    @pl.when(mine)
    def _():
        own_rows.wait()

    dx, dy = xy(f, s)
    own_half = w.at[dx, pl.ds(half + 2 * keep_half, 2), dy]
    go(own_half, own_half, S_W, ag1.at[1], dev_fs(m4(f + 2), s))
    own, _ = piece(0, 0)
    go(own, own, S_W, ag1.at[0], dev_fs(m4(f + 3 + 2 * keep_half), s))
    spread(0)
    pass_on(0, 0)

    @pl.loop(0, NX)
    def _(i):
        got(p_recv.at[1, i], rsp.at[NX + i], partner)
        for j in range(8):
            t_keep[i, j] += p_recv[1, i, j].astype(F32)

    def chunk(i):
        got(given.at[i, pl.ds(0, 4)], rsz.at[i], down)
        got(given.at[i, pl.ds(4, 4)], rsz.at[NX + i], up)
        for dy in range(NY):
            df, ds = xy(i, dy)
            for dz in range(NZH):
                total = t_keep[i, 2 * dy + dz] + given[i, 2 * dy + dz].astype(F32)
                t_keep[i, 2 * dy + dz] = total
                p[df, ds, dz] = total.astype(BF16)

            @pl.when(df != f)
            def _():
                go(p.at[df, ds], r1.at[3 - m4(df - f + 4), ds], S_RS1, rs1, dev_fs(df, s))

    chunk(0)
    for n in (1, 2):
        got(piece(n, 0)[0], ag1.at[n - 1], partner)
        spread(n)
        along_z(n, 0)
        pass_on(n, 0)

    def beside(n, m):
        at, _ = piece(n, m)
        got(at, ag2.at[4 * n + m], s_devs[m])
        if m == (3, 1, 3)[n]:
            go(at, at, S_W, ag2.at[4 * n + 2], s_devs[4 - m])
        along_z(n, m)
        pass_on(n, m)

    chunk(1)
    beside(0, 3)
    beside(0, 1)
    beside(1, 1)
    beside(1, 3)
    beside(2, 3)
    beside(2, 1)
    chunk(2)
    beside(0, 2)
    chunk(3)
    beside(1, 2)
    beside(2, 2)

    def from_z(n, m):
        got(piece(n, m, 1)[0], agzz.at[4 * (n - 1) + m], down if n == 1 and m != 2 else up)
        pass_on(n, m, 1)

    for m in (0, 3, 1):
        from_z(1, m)
        from_z(2, m)

    far = pl.ds(4 - half, 4)
    rows2 = 256
    lg[...] = jnp.zeros_like(lg)
    row_sum[...] = jnp.zeros_like(row_sum)

    def features(dx):
        got(w.at[dx, far], agp.at[dx], partner)
        columns = pl.ds(pl.multiple_of(dx * 512, 512), 512)

        @pl.loop(0, tokens // rows2)
        def _(i):
            block = pl.ds(pl.multiple_of(i * rows2, rows2), rows2)
            grad = lax.dot_general(
                grads[block, :], w[dx].reshape(512, key), (((1,), (1,)), ((), ())),
                preferred_element_type=F32,
            )
            gs[block, columns] = grad
            prod = grad * (act[block, columns].astype(F32) * inv[block, :][:, :1])
            lg[:, columns] += jnp.sum(prod.reshape(rows2 // 8, 8, 512), axis=0)
            prod = prod * gain[:, columns]
            row_sum[block, :] += (prod[:, 0:128] + prod[:, 128:256]) + (prod[:, 256:384] + prod[:, 384:512])

    me = (x * NY + y) * 2 + core

    def block(k):
        there = m4(x + k)
        features(there)
        g_send[k] = jnp.sum(
            lg[:, pl.ds(pl.multiple_of(there * 512, 512), 512)], axis=0, keepdims=True
        )
        for away in plane:
            if away[0] == k:
                go(g_send.at[k], g_recv.at[me], S_GX, gx, plane_dev(*away))

    block(0)
    g_recv[me] = g_send[0]

    from_z(1, 2)
    from_z(2, 2)

    got(r1, rs1, partner)
    for i in range(NY):
        dx, dy = xy(f, i)
        for dz in range(NZH):
            u[i, dz] = (t_keep[dx, 2 * dy + dz] + r1[0, i, dz].astype(F32)) + (
                r1[1, i, dz].astype(F32) + r1[2, i, dz].astype(F32)
            )
    for k in (1, 3, 2):
        go(u.at[m4(s + k)], u_recv.at[3 - k], S_RS2, rs2, dev_fs(f, m4(s + k)))

    block(2)
    block(1)
    block(3)

    got(u_recv, rs2, partner)
    for dz in range(NZH):
        v[dz] = (u[s, dz] + u_recv[0, dz]) + (u_recv[1, dz] + u_recv[2, dz])

    lane = lax.broadcasted_iota(jnp.int32, (24, 128), 1)
    z_there = []
    for dz in range(NZH):
        for pair in range(2):
            top = v[dz, 0:24, 128 * pair : 128 * (pair + 1)]
            low = v[dz, 24:48, 128 * pair : 128 * (pair + 1)]
            z_send[4 * dz + 2 * pair] = jnp.where(lane < 64, top, pltpu.roll(low, 64, 1))
            z_send[4 * dz + 2 * pair + 1] = jnp.where(lane < 64, pltpu.roll(top, 64, 1), low)
            z_there += [NZL * dz + half_keep + 2 * pair, NZL * dz + half_keep + 2 * pair + 1]
    z_slot = lax.div(z, 2)
    pl.semaphore_wait(far_sem, 2)
    for i in (7, 0, 6, 1, 5, 2, 4, 3):
        @pl.when(z_there[i] != z)
        def _():
            go(z_send.at[i], z_recv.at[z_slot], S_ZT, zsem, dev(x, y, z_there[i], core))

        @pl.when(z_there[i] == z)
        def _():
            z_recv[z_slot] = z_send[i]

    def inputs(i):
        @pl.loop(0, quarter // 64)
        def _(j):
            block = pl.ds(pl.multiple_of(i * quarter + j * 64, 64), 64)
            r = inv[block, :][:, :1]
            mean = jnp.sum(row_sum[block, :], axis=1, keepdims=True) * (1.0 / model)
            normed = act[block, :].astype(F32) * r
            out[block, :] = (r * (gain[...] * gs[block, :] - normed * mean)).astype(BF16)

    got(g_recv.at[pl.ds(0, 31)], gx, partner)
    line = g_recv[0]
    for i in range(1, 32):
        line = line + g_recv[i]
    for pair in range(NZL // 2):
        value = line[:, 128 * pair : 128 * (pair + 1)]
        for dz in range(NZH):
            gz_send[dz * NZL + 2 * pair] = value
            gz_send[dz * NZL + 2 * pair + 1] = value
    for k in Z_ORDER:
        there = lax.rem(z + k, NZ)
        go(gz_send.at[there], gz_recv.at[z], S_GZ, gz, dev(x, y, there, core))
    gz_recv[z] = gz_send[z]

    inputs(0)
    inputs(1)
    inputs(2)
    inputs(3)

    @pl.when(to_self)
    def _():
        got(z_recv.at[pl.ds(0, 7)], zsem, partner)

    @pl.when(jnp.logical_not(to_self))
    def _():
        got(z_recv, zsem, partner)

    total = z_recv[0]
    for k in range(1, 8):
        total = total + z_recv[k]
    tail[0:24] = total * (1.0 / 16)

    got(gz_recv.at[pl.ds(0, NZ - 1)], gz, partner)
    total = gz_recv[0]
    for k in range(1, NZ):
        total = total + gz_recv[k]
    total = jnp.broadcast_to(total * (1.0 / 16), (8, 128))
    tail[24:32] = jnp.where(lax.rem(zl, 2) == 1, pltpu.roll(total, 64, 1), total)

    @pl.when(mine)
    def _():
        left_here(w.at[0, pl.ds(0, 7), 0], S_Z)

    left_here(p_send, S_P)
    left_here(w.at[pl.ds(0, 3), pl.ds(0, 5)], S_W)
    left_here(w.at[:, pl.ds(0, 4)], S_PASS)
    left_here(p.at[pl.ds(0, 3)], S_RS1)
    left_here(give, S_ZP)
    left_here(u.at[pl.ds(0, 3)], S_RS2)

    @pl.when(to_self)
    def _():
        left_here(z_send.at[pl.ds(0, 7)], S_ZT)

    @pl.when(jnp.logical_not(to_self))
    def _():
        left_here(z_send, S_ZT)

    left_here(g_recv.at[pl.ds(0, 31)], S_GX)
    left_here(gz_send.at[pl.ds(0, NZ - 1)], S_GZ)


def finish(raw, tail, out, weight_grads, gain_grads, buf, come, leave):
    rows = raw.shape[0] // leave.shape[0]
    away = [
        pltpu.make_async_copy(raw.at[pl.ds(i * rows, rows)], out.at[pl.ds(i * rows, rows)], leave.at[i])
        for i in range(leave.shape[0])
    ]
    for made in away:
        made.start()
    into = pltpu.make_async_copy(tail, buf, come)
    into.start()
    into.wait()
    weight_grads[0:24] = buf[0:24, 0:64]
    weight_grads[24:48] = buf[0:24, 64:128]
    gain_grads[...] = buf[24:25, 0:64]
    for made in away:
        made.wait()


def local(activations, norm_gain, key_weight, key_grads):
    tokens, model = activations.shape
    key = key_grads.shape[1]
    dma = pltpu.SemaphoreType.DMA
    scratch = [
        pltpu.VMEM((tokens, model), BF16),
        pltpu.VMEM((1, model), F32),
        pltpu.VMEM((tokens, key), BF16),
        pltpu.VMEM((tokens, model), F32),
        pltpu.VMEM((tokens, 128), F32),
        pltpu.VMEM((tokens, model), BF16),
        pltpu.VMEM((tokens, 128), F32),
        pltpu.VMEM((16, 48, tokens), BF16),
        pltpu.VMEM((NX, NZL, 4, 16, key), BF16),
        pltpu.VMEM((16, 48, 256), F32),
        pltpu.VMEM((NX, 8, 48, 256), F32),
        pltpu.VMEM((NX, 8, 48, 256), F32),
        pltpu.VMEM((2, NX, 8, 48, 256), BF16),
        pltpu.VMEM((2, NX, 8, 48, 256), BF16),
        pltpu.VMEM((NX, 8, 48, 256), BF16),
        pltpu.VMEM((NX, 8, 48, 256), BF16),
        pltpu.VMEM((4, 4, NZH, 48, 256), BF16),
        pltpu.VMEM((3, 4, NZH, 48, 256), BF16),
        pltpu.VMEM((4, NZH, 48, 256), F32),
        pltpu.VMEM((3, NZH, 48, 256), F32),
        pltpu.VMEM((NZH, 48, 256), F32),
        pltpu.VMEM((8, 24, 128), F32),
        pltpu.VMEM((8, 24, 128), F32),
        pltpu.VMEM((8, model), F32),
        pltpu.VMEM((NX, 1, 512), F32),
        pltpu.VMEM((32, 1, 512), F32),
        pltpu.VMEM((NZ, 1, 128), F32),
        pltpu.VMEM((NZ, 1, 128), F32),
        dma((7,)),
        dma((10,)),
        dma((4,)),
        dma((2,)),
        dma((12,)),
        dma((8,)),
        dma((NX,)),
        dma((2 * NX,)),
        dma((2 * NX,)),
        dma,
        dma,
        dma,
        dma,
        dma,
        pltpu.SemaphoreType.REGULAR,
    ]
    vmem = pl.BlockSpec(memory_space=pltpu.VMEM)
    hbm = pl.BlockSpec(memory_space=pl.ANY)
    raw, tail = pl.pallas_call(
        kernel,
        out_shape=(
            pltpu.VMEM((tokens, model), BF16),
            pltpu.VMEM((32, 128), F32),
        ),
        in_specs=[hbm] * 4,
        out_specs=(vmem, vmem),
        scratch_shapes=scratch,
        compiler_params=pltpu.CompilerParams(
            collective_id=0, has_side_effects=True, vmem_limit_bytes=64900000
        ),
    )(activations, norm_gain.reshape(1, model), key_weight.reshape(4, 16, key), key_grads)
    input_grads, weight_grads, gain_grads = pl.pallas_call(
        finish,
        out_shape=(
            jax.ShapeDtypeStruct((tokens, model), BF16),
            jax.ShapeDtypeStruct((48, 64), F32),
            jax.ShapeDtypeStruct((1, 64), F32),
        ),
        in_specs=[hbm, hbm],
        out_specs=(hbm, vmem, vmem),
        scratch_shapes=[pltpu.VMEM((32, 128), F32), dma, dma((4,))],
        compiler_params=pltpu.CompilerParams(vmem_limit_bytes=1024 * 1024),
    )(raw, tail)
    return input_grads, weight_grads.T, gain_grads[0]


def solution(mesh):
    return jax.shard_map(
        local,
        mesh=mesh,
        in_specs=(P(("grp", "sub"), None), P(), P("sub", None), P(("grp", "sub"), None)),
        out_specs=(P(("grp", "sub"), None), P("sub", "grp"), P("sub")),
        check_vma=False,
    )
```
